1024 devices in a mesh: cores: 128 (over z_hi, y, x, core), face: 8 (over z_lo).
Axes of the slice: x: 4, y: 8, z: 16 (z_hi: 2, z_lo: 8; z = z_hi * 8 + z_lo), core: 2. Of those that a mesh axis runs over, the one named last changes fastest.
Arguments:
- fields: bfloat16 [2, 256, 32, 128, 256], P(None, 'cores', 'face'), may hold values from -6 to 6
- pore_mask: int32 [256, 32, 128], P('cores', 'face'), may hold values 0 or 1
- conv_kernel: bfloat16 [54, 32], replicated, may hold values from -0.875 to 0.875
- conv_bias: float32 [32], replicated, may hold values from -3 to 3
- read_weight: float32 [32], replicated, may hold values from -1 to 1
- obs_cells: int32 [65536], P(('cores', 'face')), may hold values from 0 to 1023
- obs_values: float32 [65536], P(('cores', 'face')), may hold values from 0 to 1
- obs_sigma: float32 [65536], P(('cores', 'face')), may hold values from 0.3 to 3
Outputs:
- analysis: bfloat16 [3, 256, 32, 128, 256], P(None, 'cores', 'face')
The draws below stay inside these ranges and needn't reach their ends.
Inputs may be any that keep to these rules, and one draw needn't show every extreme that they name: obs_cells holds the index (z * 4 + x) * 128 + y of a cell in the block of the device that holds the observation.
All inputs are finite; a program needn't handle non-finite values. No bound on the sum of `pore_mask` on one device may be relied on, other than what follows from the above.
Results may differ from the reference program's by a relative error of at most 0.0091.
Values may be sent and summed in bfloat16 or wider, within the bound.
A program may use at most 32 MiB of HBM per device.

```python
import math
import jax
import jax.numpy as jnp
from jax import lax

MEM = 256
CH = 32
CZ = 2
CX = 4
CY = 128
OBS = 64
CELLS_CORE_AXIS = 256
CELLS_FIRST_DIM = 32
NOBS = 65536
N_FACE = 8


def plant(array, key, smallest, largest):
    shape = array.shape
    index_at = [jax.random.randint(jax.random.fold_in(key, axis), (), 0, shape[axis]) for axis in range(len(shape))]
    array = array.at[tuple(index_at)].set(smallest)
    longest = shape.index(max(shape))
    index_at[longest] = (index_at[longest] + 1) % shape[longest]
    return array.at[tuple(index_at)].set(largest)


def steps_of(own_key, extent, split, smallest, top_value):
    loudness = 1.0
    for dim, shards_of in split:
        draws = jax.random.uniform(jax.random.fold_in(jax.random.fold_in(own_key, 6), dim), (shards_of,), jnp.float32, smallest / len(split), top_value / len(split))
        loudness = loudness * jnp.repeat(jnp.exp(draws), extent[dim] // shards_of).reshape((-1,) + (1,) * (len(extent) - 1 - dim))
    return loudness


def centred(stream_key, shape, width, most, cuts=(), kind=jnp.bfloat16):
    entries = width * jax.random.normal(stream_key, shape, jnp.float32)
    if cuts:
        entries = entries * steps_of(stream_key, shape, cuts, -0.22, 0.18)
    return jnp.clip(entries, -most, most).astype(kind)


def setup_inputs(seed: int = 0) -> dict:
    key_of = jax.random.split(jax.random.key(seed), 9)
    fields = centred(key_of[0], (2, CELLS_CORE_AXIS, CELLS_FIRST_DIM, CY, MEM), 1.0, 6.0, ((1, 128), (2, 8)))
    pore_mask = plant((jax.random.randint(key_of[1], (CELLS_CORE_AXIS, CELLS_FIRST_DIM, CY), 0, 4) < 3).astype(jnp.int32), jax.random.fold_in(key_of[1], 1), 0, 1)
    conv_kernel = centred(key_of[2], (54, CH), 54 ** -0.5, 0.875)
    conv_bias = centred(key_of[3], (CH,), 0.5, 3.0, (), jnp.float32)
    read_weight = centred(key_of[4], (CH,), CH ** -0.5, 1.0, (), jnp.float32)
    obs_cells = plant(jax.random.randint(key_of[5], (NOBS,), 0, CZ * CX * CY), jax.random.fold_in(key_of[5], 1), 0, (CZ * CX * CY) - 1).astype(jnp.int32)
    obs_values = jnp.clip(1.0 * jax.random.uniform(key_of[6], (NOBS,), jnp.float32) ** steps_of(key_of[6], (NOBS,), ((0, 1024),), -0.2, 0.2), 0.0, 1.0)
    obs_sigma = jnp.clip(jnp.exp(math.log(3.0) - 2.3025851 * jax.random.uniform(key_of[7], (NOBS,), jnp.float32) ** steps_of(key_of[7], (NOBS,), ((0, 1024),), -0.2, 0.2)), 0.3, 3.0)
    return {"fields": fields, "pore_mask": pore_mask, "conv_kernel": conv_kernel, "conv_bias": conv_bias, "read_weight": read_weight, "obs_cells": obs_cells, "obs_values": obs_values, "obs_sigma": obs_sigma}


def ensemble_terms(predicted, obs_values, obs_sigma):
    members = predicted.shape[1]
    root_count = math.sqrt(members - 1)
    center = lax.optimization_barrier(jnp.mean(predicted, axis=1))
    spread = predicted - center[:, None]
    inverse_sigma = 1.0 / obs_sigma
    scaled = spread * (inverse_sigma / root_count)[:, None]
    innovation = (obs_values - center) * inverse_sigma
    gram_part = jnp.einsum('om,on->mn', scaled, scaled, precision=lax.Precision.HIGHEST)
    coeff_part = jnp.einsum('om,o->m', scaled, innovation, precision=lax.Precision.HIGHEST) / root_count
    return (gram_part, coeff_part)

def finish_mixing(gram_sum, coeff_sum):
    members = gram_sum.shape[0]
    identity = jnp.eye(members, dtype=jnp.float32)
    lower_factor = jnp.linalg.cholesky(gram_sum + identity)
    transform = jax.scipy.linalg.solve_triangular(lower_factor, identity, lower=True, trans='T')
    mean_weights = jax.scipy.linalg.cho_solve((lower_factor, True), coeff_sum)
    return (transform + mean_weights[:, None]).astype(jnp.bfloat16)

def blend_state(state, mixing):
    members = state.shape[-1]
    state_float = state.astype(jnp.float32)
    state_mean = lax.optimization_barrier(jnp.mean(state_float, axis=-1, keepdims=True))
    anomalies = (state_float - state_mean).astype(jnp.bfloat16)
    moved = jnp.dot(anomalies.reshape(-1, members).astype(jnp.float32), mixing.astype(jnp.float32), preferred_element_type=jnp.float32)
    return (state_mean + moved.reshape(state.shape)).astype(jnp.bfloat16)

def reference(fields, pore_mask, conv_kernel, conv_bias, read_weight, obs_cells, obs_values, obs_sigma):
    wrapped = jnp.concatenate([fields[:, -1:], fields, fields[:, :1]], axis=1)
    padded = jnp.pad(wrapped, ((0, 0), (0, 0), (1, 1), (1, 1), (0, 0)))
    mask_float = pore_mask.astype(jnp.float32)
    kernel_float = conv_kernel.astype(jnp.float32)
    zero_index = jnp.int32(0)

    def prior_row(current_row):
        plane_index = (current_row // CELLS_FIRST_DIM).astype(jnp.int32)
        column_index = (current_row % CELLS_FIRST_DIM).astype(jnp.int32)
        window = lax.dynamic_slice(padded, (zero_index, plane_index, column_index, zero_index, zero_index), (2, 3, 3, CY + 2, MEM))
        stencil_taps = jnp.stack([window[:, :, :, offset:offset + CY, :] for offset in range(3)], axis=3).reshape(54, CY * MEM)
        hidden = jnp.einsum('kc,kn->cn', kernel_float, stencil_taps.astype(jnp.float32), precision=lax.Precision.HIGHEST)
        hidden = jax.nn.silu(hidden + conv_bias[:, None])
        logits_sat = jnp.einsum('c,cn->n', read_weight, hidden, precision=lax.Precision.HIGHEST)
        row_mask = lax.dynamic_slice(mask_float, (plane_index, column_index, zero_index), (1, 1, CY)).reshape(CY, 1)
        return (jax.nn.sigmoid(logits_sat).reshape(CY, MEM) * row_mask).astype(jnp.bfloat16)
    finished_rows = lax.map(prior_row, jnp.arange(CELLS_CORE_AXIS * CELLS_FIRST_DIM, dtype=jnp.int32))
    saturation = finished_rows.reshape(CELLS_CORE_AXIS, CELLS_FIRST_DIM, CY, MEM)
    owner = jnp.arange(NOBS, dtype=jnp.int32) // OBS
    core_slot = owner // N_FACE
    face_slot = owner % N_FACE
    plane_of = core_slot * CZ + obs_cells // (CX * CY)
    column_of = face_slot * CX + obs_cells // CY % CX
    lane_of = obs_cells % CY
    predicted = saturation[plane_of, column_of, lane_of].astype(jnp.float32)
    gram_sum, coeff_sum = ensemble_terms(predicted, obs_values, obs_sigma)
    mixing = finish_mixing(gram_sum, coeff_sum)

    def update_plane(plane_index):
        part_fields = lax.dynamic_index_in_dim(fields, plane_index, 1, keepdims=False)
        part_sat = lax.dynamic_index_in_dim(saturation, plane_index, 0, keepdims=True)
        state = jnp.concatenate([part_fields, part_sat], axis=0)
        return blend_state(state, mixing)
    planes_done = lax.map(update_plane, jnp.arange(CELLS_CORE_AXIS, dtype=jnp.int32))
    return jnp.moveaxis(planes_done, 0, 1)
```

```python
import functools
import math

import jax
import jax.numpy as jnp
import numpy as np
from jax import lax
from jax.experimental import pallas as pl
from jax.experimental.pallas import tpu as pltpu
from jax.sharding import PartitionSpec as P

MESH = pl.DeviceIdType.MESH
HIGHEST = lax.Precision.HIGHEST
F32 = jnp.float32
BF16 = jnp.bfloat16
VMEM = pl.BlockSpec(memory_space=pltpu.VMEM)
SMEM = pl.BlockSpec(memory_space=pltpu.SMEM)

CH = 32
CZ, CX, CY, MEM = 2, 4, 128, 256
CELLS = CZ * CX * CY
OBS = 64
TAPS = 54
ROWS = 2 * (CZ + 2) * (CX + 2)
PITCH = 144
HEAD = 8
DEPTH = 4 * ROWS
OUTS = 2 * CZ * CX
ROOT = math.sqrt(MEM - 1)


def tap_selection():
    chosen = np.zeros((OUTS, TAPS, 256), np.float32)
    for yo in range(2):
        for zo in range(CZ):
            for xo in range(CX):
                for f in range(2):
                    for a in range(3):
                        for b in range(3):
                            for c in range(3):
                                row = (f * (CZ + 2) + zo + a) * (CX + 2) + xo + b
                                chosen[
                                    (yo * CZ + zo) * CX + xo,
                                    27 * f + 9 * a + 3 * b + c,
                                    (yo + c) * ROWS + row,
                                ] = 1.0
    return chosen


def with_halo(cells, sides, width, closed):
    for axis, dim in sides:
        count = lax.axis_size(axis)
        ends = count if closed else count - 1
        head = lax.slice_in_dim(cells, 0, width, axis=dim)
        tail = lax.slice_in_dim(cells, cells.shape[dim] - width, cells.shape[dim], axis=dim)
        return (
            lax.ppermute(tail, axis, [(i, (i + 1) % count) for i in range(ends)]),
            lax.ppermute(head, axis, [((i + 1) % count, i) for i in range(ends)]),
        )


def forecast_kernel(
    fields, zlo, zhi, xlo, xhi, mask, chosen, kernel_t, bias, read, cells, values, sigma,
    sat_out, gram_out,
    padded_0, padded_1, rows_0, rows_1, weights, sat_0, sat_1, predicted,
):
    def place(row, block):
        block = block.astype(F32)
        padded_0[pl.ds(row * PITCH + HEAD, CY), :] = block[:, 0:128]
        padded_1[pl.ds(row * PITCH + HEAD, CY), :] = block[:, 128:256]

    def slot(f, z, x):
        return (f * (CZ + 2) + z) * (CX + 2) + x

    blank = jnp.zeros((8, 128), F32)
    for row in range(ROWS):
        for padded in (padded_0, padded_1):
            padded[pl.ds(row * PITCH, 8), :] = blank
            padded[pl.ds(row * PITCH + HEAD + CY, 8), :] = blank
    for f in range(2):
        for x in range(CX):
            for z in range(CZ):
                place(slot(f, z + 1, x + 1), fields[f, z, x])
            place(slot(f, 0, x + 1), zlo[f, 0, x])
            place(slot(f, CZ + 1, x + 1), zhi[f, 0, x])
        for z in range(CZ + 2):
            place(slot(f, z, 0), xlo[f, z, 0])
            place(slot(f, z, CX + 1), xhi[f, z, 0])

    taps = kernel_t[...]
    for out in range(OUTS):
        piece = jnp.dot(taps, chosen[out], preferred_element_type=F32)
        rows_0[pl.ds(out * CH, CH), :] = piece[:, 0:128]
        rows_1[pl.ds(out * CH, CH), :] = piece[:, 128:256]
    lane = lax.broadcasted_iota(jnp.int32, (OUTS, 16), 1)
    for c in range(CH):
        own = pl.ds(c * OUTS, OUTS)
        every = pl.ds(c, OUTS, stride=CH)
        weights[own, 0:128] = (rows_0[every, :] * 0.5).astype(BF16)
        weights[own, 128:256] = (rows_1[every, :] * 0.5).astype(BF16)
        whole = jnp.full((OUTS, 16), bias[c] * 0.5, F32)
        high = whole.astype(BF16).astype(F32)
        middle = (whole - high).astype(BF16).astype(F32)
        low = whole - high - middle
        split = jnp.where(
            lane == 0, high, jnp.where(lane == 1, middle, jnp.where(lane == 2, low, 0.0))
        )
        weights[own, DEPTH : DEPTH + 16] = split.astype(BF16)

    ones = jnp.ones((256 - DEPTH, 128), F32)

    def step(t, carry):
        halves = []
        for padded in (padded_0, padded_1):
            planes = [
                padded[pl.ds(HEAD - 1 + 2 * t + q, ROWS, stride=PITCH), :] for q in range(4)
            ]
            halves.append(jnp.concatenate(planes + [ones], axis=0).astype(BF16))
        inputs = jnp.concatenate(halves, axis=1)
        half = jnp.dot(weights[...], inputs, preferred_element_type=F32)
        total = jnp.zeros((OUTS, MEM), F32)
        for c in range(CH):
            h = half[c * OUTS : (c + 1) * OUTS]
            total = total + read[c] * (h + h * jnp.tanh(h))
        level = 0.5 + 0.5 * jnp.tanh(0.5 * total)
        for yo in range(2):
            cells_of = pl.ds(2 * t + yo, CZ * CX, stride=CY)
            sat_0[cells_of, :] = level[yo * 8 : yo * 8 + 8, 0:128]
            sat_1[cells_of, :] = level[yo * 8 : yo * 8 + 8, 128:256]
        return carry

    lax.fori_loop(0, CY // 2, step, 0)

    columns = mask[...].astype(F32)
    for zx in range(CZ * CX):
        own = pl.ds(zx * CY, CY)
        for lane_0, sat in ((0, sat_0), (128, sat_1)):
            rounded = (sat[own, :] * columns[:, zx : zx + 1]).astype(BF16)
            sat_out[own, lane_0 : lane_0 + 128] = rounded
            sat[own, :] = rounded.astype(F32)

    for o in range(OBS):
        predicted[pl.ds(o, 1), 0:128] = sat_0[pl.ds(cells[o], 1), :]
        predicted[pl.ds(o, 1), 128:256] = sat_1[pl.ds(cells[o], 1), :]
    diagonal = lax.broadcasted_iota(jnp.int32, (OBS, OBS), 0) == lax.broadcasted_iota(
        jnp.int32, (OBS, OBS), 1
    )

    def column(row):
        return jnp.sum(jnp.where(diagonal, row[...], 0.0), axis=1, keepdims=True)

    inverse_sigma = 1.0 / column(sigma)
    pred = predicted[...]
    center = jnp.sum(pred, axis=1, keepdims=True) * (1.0 / MEM)
    scaled = (pred - center) * (inverse_sigma * (1.0 / ROOT))
    innovation = (column(values) - center) * inverse_sigma
    gram = lax.dot_general(
        scaled, scaled, (((0,), (0,)), ((), ())), precision=HIGHEST, preferred_element_type=F32
    )
    coeff = jnp.sum(scaled * innovation, axis=0, keepdims=True) * (1.0 / ROOT)
    gram_out[0:MEM, :] = gram[:, 0:128]
    gram_out[MEM : 2 * MEM, :] = gram[:, 128:256]
    gram_out[MEM : MEM + 1, :] = coeff[:, 0:128]
    gram_out[MEM + 1 : MEM + 2, :] = coeff[:, 128:256]


def forecast(fields, zlo, zhi, xlo, xhi, mask, kernel, bias, read, cells, values, sigma):
    chosen = jnp.asarray(tap_selection(), BF16)
    return pl.pallas_call(
        forecast_kernel,
        out_shape=(
            jax.ShapeDtypeStruct((CELLS, MEM), BF16),
            jax.ShapeDtypeStruct((2 * MEM, 128), F32),
        ),
        in_specs=[VMEM] * 8 + [SMEM] * 3 + [VMEM] * 2,
        out_specs=(VMEM, VMEM),
        scratch_shapes=[
            pltpu.VMEM((ROWS * PITCH, 128), F32),
            pltpu.VMEM((ROWS * PITCH, 128), F32),
            pltpu.VMEM((OUTS * CH, 128), F32),
            pltpu.VMEM((OUTS * CH, 128), F32),
            pltpu.VMEM((OUTS * CH, 256), BF16),
            pltpu.VMEM((CELLS, 128), F32),
            pltpu.VMEM((CELLS, 128), F32),
            pltpu.VMEM((OBS, MEM), F32),
        ],
        compiler_params=pltpu.CompilerParams(vmem_limit_bytes=48 << 20),
        name="forecast",
    )(
        fields, zlo, zhi, xlo, xhi,
        mask.reshape(CZ * CX, CY).T, chosen, kernel.T, bias, read, cells,
        values.reshape(1, OBS), sigma.reshape(1, OBS),
    )


def total_kernel(
    part, out, from_a, from_b, from_c, sum_a, sum_b, whole,
    send_a, recv_a, send_b, recv_b, send_c, recv_c, send_d, recv_d, send_e, recv_e,
):
    cores = lax.axis_index("cores")
    face = lax.axis_index("face")
    a = lax.rem(cores, 8)
    y = lax.rem(cores // 8, 8)
    high = cores // 64
    z = high * 8 + face

    def peer_a(d):
        return (cores - a + lax.rem(a + d, 8), face)

    def peer_b(d):
        return (high * 64 + lax.rem(y + d, 8) * 8 + a, face)

    def peer_c(d):
        other = lax.rem(z + d, 16)
        return (other // 8 * 64 + lax.rem(cores, 64), lax.rem(other, 8))

    barrier = pltpu.get_barrier_semaphore()
    for d in range(1, 8):
        pl.semaphore_signal(barrier, inc=1, device_id=peer_a(d), device_id_type=MESH)
        pl.semaphore_signal(barrier, inc=1, device_id=peer_b(d), device_id_type=MESH)
    for d in range(1, 16):
        pl.semaphore_signal(barrier, inc=1, device_id=peer_c(d), device_id_type=MESH)
    pl.semaphore_wait(barrier, 29)

    def send(src, dst, sems, d, peer):
        copy = pltpu.make_async_remote_copy(
            src_ref=src, dst_ref=dst, send_sem=sems[0].at[d], recv_sem=sems[1].at[d],
            device_id=peer, device_id_type=MESH,
        )
        copy.start()
        return copy

    def rows(index, size):
        return pl.ds(pl.multiple_of(index * size, size), size)

    copies = []

    def stage(make, count):
        started = [make(d) for d in range(1, count)]
        copies.extend(started)
        return started

    for copy in stage(
        lambda d: send(part.at[rows(lax.rem(a + d, 8), 64), :], from_a.at[d], (send_a, recv_a), d, peer_a(d)), 8
    ):
        pass
    started = copies[-7:]
    value = part[rows(a, 64), :]
    for d in range(1, 8):
        started[d - 1].wait_recv()
        value = value + from_a[d]
    sum_a[...] = value
    started = stage(
        lambda d: send(sum_a.at[rows(lax.rem(y + d, 8), 8), :], from_b.at[d], (send_b, recv_b), d, peer_b(d)), 8
    )
    value = sum_a[rows(y, 8), :]
    for d in range(1, 8):
        started[d - 1].wait_recv()
        value = value + from_b[d]
    sum_b[...] = value
    started = stage(lambda d: send(sum_b, from_c.at[d], (send_c, recv_c), d, peer_c(d)), 16)
    for d in range(1, 16):
        started[d - 1].wait_recv()
        value = value + from_c[d]
    mine = whole.at[rows(y, 8), :]
    mine[...] = value
    started = stage(lambda d: send(mine, mine, (send_d, recv_d), d, peer_b(d)), 8)
    for d in range(1, 8):
        started[d - 1].wait_recv()
    place = out.at[rows(a, 64), :]
    started = stage(lambda d: send(whole, place, (send_e, recv_e), d, peer_a(d)), 8)
    place[...] = whole[...]
    for d in range(1, 8):
        started[d - 1].wait_recv()
    for copy in copies:
        copy.wait_send()


def total_over_devices(part):
    sems = [pltpu.SemaphoreType.DMA((n,)) for n in (8, 8, 8, 8, 16, 16, 8, 8, 8, 8)]
    return pl.pallas_call(
        total_kernel,
        out_shape=jax.ShapeDtypeStruct(part.shape, F32),
        in_specs=[VMEM],
        out_specs=VMEM,
        scratch_shapes=[
            pltpu.VMEM((8, 64, 128), F32),
            pltpu.VMEM((8, 8, 128), F32),
            pltpu.VMEM((16, 8, 128), F32),
            pltpu.VMEM((64, 128), F32),
            pltpu.VMEM((8, 128), F32),
            pltpu.VMEM((64, 128), F32),
        ]
        + sems,
        compiler_params=pltpu.CompilerParams(collective_id=1, has_side_effects=True),
        name="total",
    )(part)


BLOCK = 32


def analysis_kernel(gram_in, fields, sat, out, gram, inverse):
    row_index = lax.broadcasted_iota(jnp.int32, (MEM, MEM), 0)
    column_index = lax.broadcasted_iota(jnp.int32, (MEM, MEM), 1)
    identity = jnp.where(row_index == column_index, 1.0, 0.0)
    gram[:, 0:128] = gram_in[0:MEM, :]
    gram[:, 128:256] = gram_in[MEM : 2 * MEM, :]
    coeff = jnp.concatenate(
        [gram_in[MEM : MEM + 1, :], gram_in[MEM + 1 : MEM + 2, :]], axis=1
    )
    gram[0:128, 128:256] = gram_in[128:256, :].T
    gram[...] = gram[...] + identity
    inverse[...] = identity

    small_row = lax.broadcasted_iota(jnp.int32, (BLOCK, 2 * BLOCK), 0)
    small_column = lax.broadcasted_iota(jnp.int32, (BLOCK, 2 * BLOCK), 1)
    for k in range(0, MEM, BLOCK):
        after = k + BLOCK
        wide = gram[k:after, :]
        corner = jnp.where(small_row + BLOCK == small_column, 1.0, 0.0)
        work = jnp.concatenate([wide[:, k:after], corner[:, BLOCK:]], axis=1)
        for i in range(BLOCK):
            pivot = work[i : i + 1, :]
            scale = pivot * (1.0 / pivot[:, i : i + 1])
            factor = jnp.where(small_row[:, 0:1] > i, work[:, i : i + 1], 0.0)
            work = work - factor * scale
        pivots = jnp.sum(jnp.where(small_row == small_column, work, 0.0), axis=1, keepdims=True)
        lower = work[:, BLOCK:] * (1.0 / jnp.sqrt(pivots))
        upper_rows = jnp.dot(lower, wide, precision=HIGHEST, preferred_element_type=F32)
        inverse_rows = jnp.dot(
            lower, inverse[k:after, :], precision=HIGHEST, preferred_element_type=F32
        )
        inverse[k:after, :] = inverse_rows
        if after < MEM:
            turned = upper_rows[:, after:]
            both = (((0,), (0,)), ((), ()))
            gram[after:, :] = gram[after:, :] - lax.dot_general(
                turned, upper_rows, both, precision=HIGHEST, preferred_element_type=F32
            )
            inverse[after:, :] = inverse[after:, :] - lax.dot_general(
                turned, inverse_rows, both, precision=HIGHEST, preferred_element_type=F32
            )

    low = jnp.where(row_index >= column_index, inverse[...], 0.0)
    half_way = jnp.sum(low * coeff, axis=1, keepdims=True)
    weights = jnp.sum(low * half_way, axis=0, keepdims=True)
    mixing_t = (low + weights).astype(BF16)

    def update(state):
        state = state.astype(F32)
        mean = jnp.sum(state, axis=1, keepdims=True) * (1.0 / MEM)
        moved = lax.dot_general(
            (state - mean).astype(BF16), mixing_t, (((1,), (1,)), ((), ())),
            preferred_element_type=F32,
        )
        return (mean + moved).astype(BF16)

    for z in range(CZ):
        for x in range(CX):
            for f in range(2):
                out[f, z, x] = update(fields[f, z, x])
            out[2, z, x] = update(sat[z, x])


def analysis(gram, fields, sat):
    return pl.pallas_call(
        analysis_kernel,
        out_shape=jax.ShapeDtypeStruct((3,) + fields.shape[1:], BF16),
        in_specs=[VMEM] * 3,
        out_specs=VMEM,
        scratch_shapes=[pltpu.VMEM((MEM, MEM), F32), pltpu.VMEM((MEM, MEM), F32)],
        compiler_params=pltpu.CompilerParams(vmem_limit_bytes=32 << 20),
        name="analysis",
    )(gram, fields, sat)


def shards(
    fields, pore_mask, conv_kernel, conv_bias, read_weight, obs_cells, obs_values, obs_sigma
):
    zlo, zhi = with_halo(fields, (("cores", 1),), 1, True)
    extended = jnp.concatenate([zlo, fields, zhi], axis=1)
    xlo, xhi = with_halo(extended, (("face", 2),), 1, False)
    sat, part = forecast(
        fields, zlo, zhi, xlo, xhi, pore_mask, conv_kernel, conv_bias, read_weight,
        obs_cells, obs_values, obs_sigma,
    )
    total = total_over_devices(part)
    return analysis(total, fields, sat.reshape(CZ, CX, CY, MEM))


def solution(mesh):
    return jax.shard_map(
        shards,
        mesh=mesh,
        in_specs=(
            P(None, "cores", "face", None, None),
            P("cores", "face", None),
            P(),
            P(),
            P(),
            P(("cores", "face")),
            P(("cores", "face")),
            P(("cores", "face")),
        ),
        out_specs=P(None, "cores", "face", None, None),
        check_vma=False,
    )
```

```python
import functools
import math

import jax
import jax.numpy as jnp
import numpy as np
from jax import lax
from jax.experimental import pallas as pl
from jax.experimental.pallas import tpu as pltpu
from jax.sharding import PartitionSpec as P

MESH = pl.DeviceIdType.MESH
HIGHEST = lax.Precision.HIGHEST
F32 = jnp.float32
BF16 = jnp.bfloat16
VMEM = pl.BlockSpec(memory_space=pltpu.VMEM)
SMEM = pl.BlockSpec(memory_space=pltpu.SMEM)

CH = 32
CZ, CX, CY, MEM = 2, 4, 128, 256
CELLS = CZ * CX * CY
OBS = 64
TAPS = 54
ROWS = 2 * (CZ + 2) * (CX + 2)
PITCH = 144
HEAD = 8
DEPTH = 4 * ROWS
OUTS = 2 * CZ * CX
ROOT = math.sqrt(MEM - 1)


def tap_selection():
    chosen = np.zeros((OUTS, TAPS, 256), np.float32)
    for yo in range(2):
        for zo in range(CZ):
            for xo in range(CX):
                for f in range(2):
                    for a in range(3):
                        for b in range(3):
                            for c in range(3):
                                row = (f * (CZ + 2) + zo + a) * (CX + 2) + xo + b
                                chosen[
                                    (yo * CZ + zo) * CX + xo,
                                    27 * f + 9 * a + 3 * b + c,
                                    (yo + c) * ROWS + row,
                                ] = 1.0
    return chosen


def exchange(
    fields, zh, xh, hop_1, hop_2, sent, z_sem, edge_sem, corner_sem, hop_sem, greet_more, more, meanwhile
):
    cores = lax.axis_index("cores")
    face = lax.axis_index("face")
    core = lax.rem(cores, 2)
    x_chip = lax.rem(cores // 2, 4)
    y_chip = lax.rem(cores // 8, 8)
    high = cores // 64
    above, below = lax.rem(cores + 1, 128), lax.rem(cores + 127, 128)
    top, bottom = lax.rem(cores, 64) == 63, lax.rem(cores, 64) == 0
    not_top, not_bottom = jnp.logical_not(top), jnp.logical_not(bottom)
    has_left, has_right = face > 0, face < 7
    partner = lax.rem(cores + 64, 128)
    first = high * 64 + core * 63
    last = high * 64 + 63 - core * 63
    is_first = cores == first
    later = jnp.logical_not(is_first)
    sends_right = lax.rem(y_chip, 4) == 3
    sends_left = lax.rem(y_chip, 4) == 0

    def both(*conditions):
        return functools.reduce(jnp.logical_and, conditions)

    barrier = pltpu.get_barrier_semaphore()

    def greet(condition, *peers):
        def signal():
            for peer in peers:
                pl.semaphore_signal(barrier, inc=1, device_id=peer, device_id_type=MESH)

        if condition is None:
            signal()
        else:
            pl.when(condition)(signal)

    def columns(core_of, rows, face_of):
        return [(high * 64 + j * 8 + i * 2 + core_of, face_of) for j in rows for i in range(4)]

    greet_more(barrier)
    greet(None, (partner, face))
    greet(later, (first, face))
    greet(not_bottom, (below, face))
    greet(not_top, (above, face))
    greet(has_left, (cores, face - 1))
    greet(has_right, (cores, face + 1))
    for end, core_of in ((bottom, 1), (top, 0)):
        greet(end, *columns(core_of, range(8), face))
        greet(both(end, has_left), *columns(core_of, (3, 7), face - 1))
        greet(both(end, has_right), *columns(core_of, (0, 4), face + 1))

    def one(condition):
        return jnp.where(condition, 1, 0)

    expected = (
        2
        + more
        + one(not_top)
        + one(not_bottom)
        + one(has_left)
        + one(has_right)
        + one(both(sends_right, has_right))
        + one(both(sends_left, has_left))
        + 31 * one(is_first)
    )
    pl.semaphore_wait(barrier, expected)

    started = []

    def send(condition, src, dst, arrived, *peer):
        copy = pltpu.make_async_remote_copy(
            src_ref=src, dst_ref=dst, send_sem=sent.at[len(started)], recv_sem=arrived,
            device_id=peer, device_id_type=MESH,
        )
        started.append((condition, copy))
        if condition is None:
            copy.start()
        else:
            pl.when(condition)(copy.start)

    def arrival(dst, arrived, *peer):
        return pltpu.make_async_remote_copy(
            src_ref=dst, dst_ref=dst, send_sem=sent.at[0], recv_sem=arrived,
            device_id=peer, device_id_type=MESH,
        )

    part = CY // 4

    def rows(quarter):
        return pl.ds(pl.multiple_of(quarter * part, part), part)

    def piece(j, i):
        return fields.at[j // 4, core, lax.rem(j, 4), rows(i), :]

    for n in range(31):
        at = n + 1 - core
        j, i = at // 4, lax.rem(at, 4)
        send(is_first, piece(j, i), hop_1, hop_sem.at[0], high * 64 + at * 2 + core, face)
    send(is_first, piece(y_chip, x_chip), hop_2, hop_sem.at[1], partner, face)
    for side, x, condition, peer in (
        (0, CX - 1, has_right, face + 1),
        (1, 0, has_left, face - 1),
    ):
        for f in range(2):
            send(condition, fields.at[f, :, x], xh.at[side, f, pl.ds(1, CZ)], edge_sem.at[side, f], cores, peer)
    pl.when(later)(arrival(hop_1, hop_sem.at[0], first, face).wait_recv)
    send(later, hop_1, hop_2, hop_sem.at[1], partner, face)
    for f in range(2):
        send(not_top, fields.at[f, CZ - 1], zh.at[0, f], z_sem.at[0, f], above, face)
        send(not_bottom, fields.at[f, 0], zh.at[1, f], z_sem.at[1, f], below, face)
    meanwhile()
    for side, condition in ((0, has_left), (1, has_right)):
        for f in range(2):
            pl.when(condition)(
                arrival(xh.at[side, f, pl.ds(1, CZ)], edge_sem.at[side, f], partner, face).wait_recv
            )
            send(both(condition, not_top), xh.at[side, f, CZ], xh.at[side, f, 0], corner_sem.at[side, f, 0], above, face)
            send(both(condition, not_bottom), xh.at[side, f, 1], xh.at[side, f, CZ + 1], corner_sem.at[side, f, 1], below, face)
    arrival(hop_2, hop_sem.at[1], partner, face).wait_recv()
    f, x = y_chip // 4, lax.rem(y_chip, 4)
    side = 1 - core
    plane = 3 * side
    send(None, hop_2, zh.at[side, f, x, rows(x_chip), :], z_sem.at[side, f], last, face)
    for to, condition, peer in (
        (0, both(sends_right, has_right), face + 1),
        (1, both(sends_left, has_left), face - 1),
    ):
        send(condition, hop_2, xh.at[to, f, plane, rows(x_chip), :], corner_sem.at[to, f, side], last, peer)

    for side, condition in ((0, has_left), (1, has_right)):
        def clear():
            xh[side] = jnp.zeros_like(xh[side])

        def wait_corners():
            for f in range(2):
                for end in range(2):
                    arrival(xh.at[side, f, 3 * end], corner_sem.at[side, f, end], partner, face).wait_recv()

        pl.when(jnp.logical_not(condition))(clear)
        for f in range(2):
            arrival(zh.at[side, f], z_sem.at[side, f], partner, face).wait_recv()
        pl.when(condition)(wait_corners)
    def finish():
        for condition, copy in started:
            if condition is None:
                copy.wait_send()
            else:
                pl.when(condition)(copy.wait_send)

    return finish


def forecast_kernel(
    fields, mask, chosen, kernel_t, bias, read, cells, values, sigma,
    sat_out, total_out,
    padded_0, padded_1, rows_0, rows_1, weights, sat_0, sat_1, predicted, part,
    zh, xh, hop_1, hop_2, sent, z_sem, edge_sem, corner_sem, hop_sem, *total_scratch,
):
    def place(row, block):
        block = block.astype(F32)
        padded_0[pl.ds(row * PITCH + HEAD, CY), :] = block[:, 0:128]
        padded_1[pl.ds(row * PITCH + HEAD, CY), :] = block[:, 128:256]

    def slot(f, z, x):
        return (f * (CZ + 2) + z) * (CX + 2) + x

    def prepare():
        own_rows()
        make_weights()

    def own_rows():
        blank = jnp.zeros((8, 128), F32)
        for row in range(ROWS):
            for padded in (padded_0, padded_1):
                padded[pl.ds(row * PITCH, 8), :] = blank
                padded[pl.ds(row * PITCH + HEAD + CY, 8), :] = blank
        for f in range(2):
            for x in range(CX):
                for z in range(CZ):
                    place(slot(f, z + 1, x + 1), fields[f, z, x])

    def make_weights():
        taps = kernel_t[...]
        for out in range(OUTS):
            piece = jnp.dot(taps, chosen[out], preferred_element_type=F32)
            rows_0[pl.ds(out * CH, CH), :] = piece[:, 0:128]
            rows_1[pl.ds(out * CH, CH), :] = piece[:, 128:256]
        lane = lax.broadcasted_iota(jnp.int32, (OUTS, 16), 1)
        for c in range(CH):
            own = pl.ds(c * OUTS, OUTS)
            every = pl.ds(c, OUTS, stride=CH)
            weights[own, 0:128] = (rows_0[every, :] * 0.5).astype(BF16)
            weights[own, 128:256] = (rows_1[every, :] * 0.5).astype(BF16)
            whole = jnp.full((OUTS, 16), bias[c] * 0.5, F32)
            high = whole.astype(BF16).astype(F32)
            middle = (whole - high).astype(BF16).astype(F32)
            low = whole - high - middle
            split = jnp.where(
                lane == 0, high, jnp.where(lane == 1, middle, jnp.where(lane == 2, low, 0.0))
            )
            weights[own, DEPTH : DEPTH + 16] = split.astype(BF16)

    greet_total, sum_over_devices = total(part, total_out, *total_scratch)
    finish = exchange(
        fields, zh, xh, hop_1, hop_2, sent, z_sem, edge_sem, corner_sem, hop_sem,
        greet_total, PEERS, prepare,
    )
    for f in range(2):
        for x in range(CX):
            place(slot(f, 0, x + 1), zh[0, f, x])
            place(slot(f, CZ + 1, x + 1), zh[1, f, x])
        for z in range(CZ + 2):
            place(slot(f, z, 0), xh[0, f, z])
            place(slot(f, z, CX + 1), xh[1, f, z])

    ones = jnp.ones((256 - DEPTH, 128), F32)

    def step(t, carry):
        halves = []
        for padded in (padded_0, padded_1):
            planes = [
                padded[pl.ds(HEAD - 1 + 2 * t + q, ROWS, stride=PITCH), :] for q in range(4)
            ]
            halves.append(jnp.concatenate(planes + [ones], axis=0).astype(BF16))
        inputs = jnp.concatenate(halves, axis=1)
        half = jnp.dot(weights[...], inputs, preferred_element_type=F32)
        total = jnp.zeros((OUTS, MEM), F32)
        for c in range(CH):
            h = half[c * OUTS : (c + 1) * OUTS]
            total = total + read[c] * (h + h * jnp.tanh(h))
        level = 0.5 + 0.5 * jnp.tanh(0.5 * total)
        for yo in range(2):
            cells_of = pl.ds(2 * t + yo, CZ * CX, stride=CY)
            sat_0[cells_of, :] = level[yo * 8 : yo * 8 + 8, 0:128]
            sat_1[cells_of, :] = level[yo * 8 : yo * 8 + 8, 128:256]
        return carry

    lax.fori_loop(0, CY // 2, step, 0, unroll=8)

    columns = mask[...].astype(F32)
    for zx in range(CZ * CX):
        own = pl.ds(zx * CY, CY)
        for lane_0, sat in ((0, sat_0), (128, sat_1)):
            rounded = (sat[own, :] * columns[:, zx : zx + 1]).astype(BF16)
            sat_out[own, lane_0 : lane_0 + 128] = rounded
            sat[own, :] = rounded.astype(F32)

    for o in range(OBS):
        predicted[pl.ds(o, 1), 0:128] = sat_0[pl.ds(cells[o], 1), :]
        predicted[pl.ds(o, 1), 128:256] = sat_1[pl.ds(cells[o], 1), :]
    diagonal = lax.broadcasted_iota(jnp.int32, (OBS, OBS), 0) == lax.broadcasted_iota(
        jnp.int32, (OBS, OBS), 1
    )

    def column(row):
        return jnp.sum(jnp.where(diagonal, row[...], 0.0), axis=1, keepdims=True)

    inverse_sigma = 1.0 / column(sigma)
    pred = predicted[...]
    center = jnp.sum(pred, axis=1, keepdims=True) * (1.0 / MEM)
    scaled = (pred - center) * (inverse_sigma * (1.0 / ROOT))
    innovation = (column(values) - center) * inverse_sigma
    gram = lax.dot_general(
        scaled, scaled, (((0,), (0,)), ((), ())), precision=HIGHEST, preferred_element_type=F32
    )
    coeff = jnp.sum(scaled * innovation, axis=0, keepdims=True) * (1.0 / ROOT)
    part[0:MEM, :] = gram[:, 0:128]
    part[MEM : 2 * MEM, :] = gram[:, 128:256]
    part[MEM : MEM + 1, :] = coeff[:, 0:128]
    part[MEM + 1 : MEM + 2, :] = coeff[:, 128:256]
    sum_over_devices()
    finish()


def forecast(fields, mask, kernel, bias, read, cells, values, sigma):
    chosen = jnp.asarray(tap_selection(), BF16)
    dma = pltpu.SemaphoreType.DMA
    return pl.pallas_call(
        forecast_kernel,
        out_shape=(
            jax.ShapeDtypeStruct((CELLS, MEM), BF16),
            jax.ShapeDtypeStruct((2 * MEM, 128), F32),
        ),
        in_specs=[VMEM] * 4 + [SMEM] * 3 + [VMEM] * 2,
        out_specs=(VMEM, VMEM),
        scratch_shapes=[
            pltpu.VMEM((ROWS * PITCH, 128), F32),
            pltpu.VMEM((ROWS * PITCH, 128), F32),
            pltpu.VMEM((OUTS * CH, 128), F32),
            pltpu.VMEM((OUTS * CH, 128), F32),
            pltpu.VMEM((OUTS * CH, 256), BF16),
            pltpu.VMEM((CELLS, 128), F32),
            pltpu.VMEM((CELLS, 128), F32),
            pltpu.VMEM((OBS, MEM), F32),
            pltpu.VMEM((2 * MEM, 128), F32),
            pltpu.VMEM((2, 2, 4, CY, MEM), BF16),
            pltpu.VMEM((2, 2, 4, CY, MEM), BF16),
            pltpu.VMEM((CY // 4, MEM), BF16),
            pltpu.VMEM((CY // 4, MEM), BF16),
            dma((56,)),
            dma((2, 2)),
            dma((2, 2)),
            dma((2, 2, 2)),
            dma((2,)),
            pltpu.VMEM((8, 64, 128), F32),
            pltpu.VMEM((8, 8, 128), F32),
            pltpu.VMEM((16, 8, 128), F32),
            pltpu.VMEM((64, 128), F32),
            pltpu.VMEM((8, 128), F32),
            pltpu.VMEM((64, 128), F32),
        ]
        + [dma((n,)) for n in (8, 8, 8, 8, 16, 16, 8, 8, 8, 8)],
        compiler_params=pltpu.CompilerParams(
            collective_id=1, has_side_effects=True, vmem_limit_bytes=40 << 20
        ),
        name="forecast",
    )(
        fields, mask.reshape(CZ * CX, CY).T, chosen, kernel.T, bias, read, cells,
        values.reshape(1, OBS), sigma.reshape(1, OBS),
    )


def total(
    part, out, from_a, from_b, from_c, sum_a, sum_b, whole,
    send_a, recv_a, send_b, recv_b, send_c, recv_c, send_d, recv_d, send_e, recv_e,
):
    cores = lax.axis_index("cores")
    face = lax.axis_index("face")
    a = lax.rem(cores, 8)
    y = lax.rem(cores // 8, 8)
    high = cores // 64
    z = high * 8 + face

    def peer_a(d):
        return (cores - a + lax.rem(a + d, 8), face)

    def peer_b(d):
        return (high * 64 + lax.rem(y + d, 8) * 8 + a, face)

    def peer_c(d):
        other = lax.rem(z + d, 16)
        return (other // 8 * 64 + lax.rem(cores, 64), lax.rem(other, 8))

    def greet(barrier):
        for d in range(1, 8):
            pl.semaphore_signal(barrier, inc=1, device_id=peer_a(d), device_id_type=MESH)
            pl.semaphore_signal(barrier, inc=1, device_id=peer_b(d), device_id_type=MESH)
        for d in range(1, 16):
            pl.semaphore_signal(barrier, inc=1, device_id=peer_c(d), device_id_type=MESH)

    def sum_over_devices():
        def send(src, dst, sems, d, peer):
            copy = pltpu.make_async_remote_copy(
                src_ref=src, dst_ref=dst, send_sem=sems[0].at[d], recv_sem=sems[1].at[d],
                device_id=peer, device_id_type=MESH,
            )
            copy.start()
            return copy

        def rows(index, size):
            return pl.ds(pl.multiple_of(index * size, size), size)

        copies = []

        def stage(make, count):
            started = [make(d) for d in range(1, count)]
            copies.extend(started)
            return started

        for copy in stage(
            lambda d: send(part.at[rows(lax.rem(a + d, 8), 64), :], from_a.at[d], (send_a, recv_a), d, peer_a(d)), 8
        ):
            pass
        started = copies[-7:]
        value = part[rows(a, 64), :]
        for d in range(1, 8):
            started[d - 1].wait_recv()
            value = value + from_a[d]
        sum_a[...] = value
        started = stage(
            lambda d: send(sum_a.at[rows(lax.rem(y + d, 8), 8), :], from_b.at[d], (send_b, recv_b), d, peer_b(d)), 8
        )
        value = sum_a[rows(y, 8), :]
        for d in range(1, 8):
            started[d - 1].wait_recv()
            value = value + from_b[d]
        sum_b[...] = value
        started = stage(lambda d: send(sum_b, from_c.at[d], (send_c, recv_c), d, peer_c(d)), 16)
        for d in range(1, 16):
            started[d - 1].wait_recv()
            value = value + from_c[d]
        mine = whole.at[rows(y, 8), :]
        mine[...] = value
        started = stage(lambda d: send(mine, mine, (send_d, recv_d), d, peer_b(d)), 8)
        for d in range(1, 8):
            started[d - 1].wait_recv()
        place = out.at[rows(a, 64), :]
        started = stage(lambda d: send(whole, place, (send_e, recv_e), d, peer_a(d)), 8)
        place[...] = whole[...]
        for d in range(1, 8):
            started[d - 1].wait_recv()
        for copy in copies:
            copy.wait_send()

    return greet, sum_over_devices


PEERS = 7 + 7 + 15


BLOCK = 128


def analysis_kernel(gram_in, fields, sat, out, gram, inverse):
    row_index = lax.broadcasted_iota(jnp.int32, (MEM, MEM), 0)
    column_index = lax.broadcasted_iota(jnp.int32, (MEM, MEM), 1)
    identity = jnp.where(row_index == column_index, 1.0, 0.0)
    gram[:, 0:128] = gram_in[0:MEM, :]
    gram[:, 128:256] = gram_in[MEM : 2 * MEM, :]
    coeff = jnp.concatenate(
        [gram_in[MEM : MEM + 1, :], gram_in[MEM + 1 : MEM + 2, :]], axis=1
    )
    gram[0:128, 128:256] = gram_in[128:256, :].T
    gram[...] = gram[...] + identity
    inverse[...] = identity

    small_row = lax.broadcasted_iota(jnp.int32, (BLOCK, 2 * BLOCK), 0)
    small_column = lax.broadcasted_iota(jnp.int32, (BLOCK, 2 * BLOCK), 1)
    odd = lax.rem(small_row[:, 0:1], 2) == 1
    corner = jnp.where(small_row + BLOCK == small_column, 1.0, 0.0)[:, BLOCK:]
    both = (((0,), (0,)), ((), ()))

    def product(left, right):
        return jnp.dot(left, right, precision=HIGHEST, preferred_element_type=F32)

    def wide(column):
        return jnp.broadcast_to(column, (column.shape[0], 2 * BLOCK))

    def down(block):
        return jnp.concatenate([block[-1:], block[:-1]], axis=0)

    for k in range(0, MEM, BLOCK):
        after = k + BLOCK
        work = jnp.concatenate([gram[k:after, k:after], corner], axis=1)
        finished = []
        for i in range(0, BLOCK, 4):
            if i and i % 8 == 0:
                finished.append(work[:8])
                work = work[8:]
            row = i % 8
            r0, r1, r2, r3 = (work[row + q : row + q + 1, :] for q in range(4))
            at = [slice(i + q, i + q + 1) for q in range(4)]
            a00, a01, a02, a03 = (wide(r0[:, at[q]]) for q in range(4))
            a11, a12, a13 = (wide(r1[:, at[q]]) for q in range(1, 4))
            a22, a23, a33 = wide(r2[:, at[2]]), wide(r2[:, at[3]]), wide(r3[:, at[3]])
            c0, c1, c2, c3 = (wide(work[:, at[q]]) for q in range(4))
            inverse_det = 1.0 / (a00 * a11 - a01 * a01)
            p00, p01, p11 = a11 * inverse_det, -a01 * inverse_det, a00 * inverse_det
            x02, x12 = p00 * a02 + p01 * a12, p01 * a02 + p11 * a12
            x03, x13 = p00 * a03 + p01 * a13, p01 * a03 + p11 * a13
            b22 = a22 - (a02 * x02 + a12 * x12)
            b23 = a23 - (a02 * x03 + a12 * x13)
            b33 = a33 - (a03 * x03 + a13 * x13)
            inverse_det = 1.0 / (b22 * b33 - b23 * b23)
            q22, q23, q33 = b33 * inverse_det, -b23 * inverse_det, b22 * inverse_det
            s0, s1 = p00 * r0 + p01 * r1, p01 * r0 + p11 * r1
            r2 = r2 - (a02 * s0 + a12 * s1)
            r3 = r3 - (a03 * s0 + a13 * s1)
            s2, s3 = q22 * r2 + q23 * r3, q23 * r2 + q33 * r3
            c2 = c2 - (c0 * x02 + c1 * x12)
            c3 = c3 - (c0 * x03 + c1 * x13)
            first = small_row[: work.shape[0]] > row + 1
            second = small_row[: work.shape[0]] > row + 3
            work = work - (
                (jnp.where(first, c0, 0.0) * s0 + jnp.where(first, c1, 0.0) * s1)
                + (jnp.where(second, c2, 0.0) * s2 + jnp.where(second, c3, 0.0) * s3)
            )
        work = jnp.concatenate(finished + [work], axis=0)
        diagonal = jnp.sum(jnp.where(small_row == small_column, work, 0.0), axis=1, keepdims=True)
        beside = jnp.sum(
            jnp.where(small_row - 1 == small_column, work, 0.0), axis=1, keepdims=True
        )
        ratio = jnp.where(odd, beside / down(diagonal), 0.0)
        pivots = diagonal - ratio * beside
        right = work[:, BLOCK:]
        lower = (right - ratio * down(right)) * (1.0 / jnp.sqrt(pivots))
        inverse_rows = product(lower, inverse[k:after, :])
        inverse[k:after, :] = inverse_rows
        if after < MEM:
            upper_rows = product(lower, gram[k:after, :])
            turned = upper_rows[:, after:]
            gram[after:, :] = gram[after:, :] - lax.dot_general(
                turned, upper_rows, both, precision=HIGHEST, preferred_element_type=F32
            )
            inverse[after:, :] = inverse[after:, :] - lax.dot_general(
                turned, inverse_rows, both, precision=HIGHEST, preferred_element_type=F32
            )

    low = jnp.where(row_index >= column_index, inverse[...], 0.0)
    half_way = jnp.sum(low * coeff, axis=1, keepdims=True)
    weights = jnp.sum(low * half_way, axis=0, keepdims=True)
    mixing_t = (low + weights).astype(BF16)

    def update(state):
        state = state.astype(F32)
        mean = jnp.sum(state, axis=1, keepdims=True) * (1.0 / MEM)
        moved = lax.dot_general(
            (state - mean).astype(BF16), mixing_t, (((1,), (1,)), ((), ())),
            preferred_element_type=F32,
        )
        return (mean + moved).astype(BF16)

    for z in range(CZ):
        for x in range(CX):
            for f in range(2):
                out[f, z, x] = update(fields[f, z, x])
            out[2, z, x] = update(sat[z, x])


def analysis(gram, fields, sat):
    return pl.pallas_call(
        analysis_kernel,
        out_shape=jax.ShapeDtypeStruct((3,) + fields.shape[1:], BF16),
        in_specs=[VMEM] * 3,
        out_specs=VMEM,
        scratch_shapes=[pltpu.VMEM((MEM, MEM), F32), pltpu.VMEM((MEM, MEM), F32)],
        compiler_params=pltpu.CompilerParams(vmem_limit_bytes=32 << 20),
        name="analysis",
    )(gram, fields, sat)


def shards(
    fields, pore_mask, conv_kernel, conv_bias, read_weight, obs_cells, obs_values, obs_sigma
):
    sat, summed = forecast(
        fields, pore_mask, conv_kernel, conv_bias, read_weight, obs_cells, obs_values, obs_sigma
    )
    return analysis(summed, fields, sat.reshape(CZ, CX, CY, MEM))


def solution(mesh):
    return jax.shard_map(
        shards,
        mesh=mesh,
        in_specs=(
            P(None, "cores", "face", None, None),
            P("cores", "face", None),
            P(),
            P(),
            P(),
            P(("cores", "face")),
            P(("cores", "face")),
            P(("cores", "face")),
        ),
        out_specs=P(None, "cores", "face", None, None),
        check_vma=False,
    )
```

```python
import functools
import math

import jax
import jax.numpy as jnp
import numpy as np
from jax import lax
from jax.experimental import pallas as pl
from jax.experimental.pallas import tpu as pltpu
from jax.sharding import PartitionSpec as P

MESH = pl.DeviceIdType.MESH
HIGHEST = lax.Precision.HIGHEST
F32 = jnp.float32
BF16 = jnp.bfloat16
VMEM = pl.BlockSpec(memory_space=pltpu.VMEM)
SMEM = pl.BlockSpec(memory_space=pltpu.SMEM)

CH = 32
CZ, CX, CY, MEM = 2, 4, 128, 256
CELLS = CZ * CX * CY
OBS = 64
TAPS = 54
ROWS = 2 * (CZ + 2) * (CX + 2)
SPAN = 40
PITCH = 144
HEAD = 8
OUTS = 4 * CX
DEPTH = 6 * SPAN
ROOT = math.sqrt(MEM - 1)


def tap_selection():
    chosen = np.zeros((OUTS, TAPS, 256), np.float32)
    for yo in range(4):
        for xo in range(CX):
            for f in range(2):
                for a in range(3):
                    for b in range(3):
                        for c in range(3):
                            row = (2 * a + f) * (CX + 2) + xo + b
                            chosen[
                                yo * CX + xo, 27 * f + 9 * a + 3 * b + c, (yo + c) * SPAN + row
                            ] = 1.0
    return chosen


def exchange(
    fields, zh, xh, hop_1, hop_2, sent, z_sem, edge_sem, corner_sem, hop_sem, greet_more, more, meanwhile
):
    cores = lax.axis_index("cores")
    face = lax.axis_index("face")
    core = lax.rem(cores, 2)
    x_chip = lax.rem(cores // 2, 4)
    y_chip = lax.rem(cores // 8, 8)
    high = cores // 64
    above, below = lax.rem(cores + 1, 128), lax.rem(cores + 127, 128)
    top, bottom = lax.rem(cores, 64) == 63, lax.rem(cores, 64) == 0
    not_top, not_bottom = jnp.logical_not(top), jnp.logical_not(bottom)
    has_left, has_right = face > 0, face < 7
    partner = lax.rem(cores + 64, 128)
    first = high * 64 + core * 63
    last = high * 64 + 63 - core * 63
    is_first = cores == first
    later = jnp.logical_not(is_first)
    sends_right = lax.rem(y_chip, 4) == 3
    sends_left = lax.rem(y_chip, 4) == 0

    def both(*conditions):
        return functools.reduce(jnp.logical_and, conditions)

    barrier = pltpu.get_barrier_semaphore()

    def greet(condition, *peers):
        def signal():
            for peer in peers:
                pl.semaphore_signal(barrier, inc=1, device_id=peer, device_id_type=MESH)

        if condition is None:
            signal()
        else:
            pl.when(condition)(signal)

    def columns(core_of, rows, face_of):
        return [(high * 64 + j * 8 + i * 2 + core_of, face_of) for j in rows for i in range(4)]

    greet_more(barrier)
    greet(None, (partner, face))
    greet(later, (first, face))
    greet(not_bottom, (below, face))
    greet(not_top, (above, face))
    greet(has_left, (cores, face - 1))
    greet(has_right, (cores, face + 1))
    for end, core_of in ((bottom, 1), (top, 0)):
        greet(end, *columns(core_of, range(8), face))
        greet(both(end, has_left), *columns(core_of, (3, 7), face - 1))
        greet(both(end, has_right), *columns(core_of, (0, 4), face + 1))

    def one(condition):
        return jnp.where(condition, 1, 0)

    expected = (
        2
        + more
        + one(not_top)
        + one(not_bottom)
        + one(has_left)
        + one(has_right)
        + one(both(sends_right, has_right))
        + one(both(sends_left, has_left))
        + 31 * one(is_first)
    )
    pl.semaphore_wait(barrier, expected)

    started = []

    def send(condition, src, dst, arrived, *peer):
        copy = pltpu.make_async_remote_copy(
            src_ref=src, dst_ref=dst, send_sem=sent.at[len(started)], recv_sem=arrived,
            device_id=peer, device_id_type=MESH,
        )
        started.append((condition, copy))
        if condition is None:
            copy.start()
        else:
            pl.when(condition)(copy.start)

    def arrival(dst, arrived, *peer):
        return pltpu.make_async_remote_copy(
            src_ref=dst, dst_ref=dst, send_sem=sent.at[0], recv_sem=arrived,
            device_id=peer, device_id_type=MESH,
        )

    part = CY // 4

    def rows(quarter):
        return pl.ds(pl.multiple_of(quarter * part, part), part)

    def piece(j, i):
        return fields.at[j // 4, core, lax.rem(j, 4), rows(i), :]

    for n in range(31):
        at = n + 1 - core
        j, i = at // 4, lax.rem(at, 4)
        send(is_first, piece(j, i), hop_1, hop_sem.at[0], high * 64 + at * 2 + core, face)
    send(is_first, piece(y_chip, x_chip), hop_2, hop_sem.at[1], partner, face)
    for side, x, condition, peer in (
        (0, CX - 1, has_right, face + 1),
        (1, 0, has_left, face - 1),
    ):
        for f in range(2):
            send(condition, fields.at[f, :, x], xh.at[side, f, pl.ds(1, CZ)], edge_sem.at[side, f], cores, peer)
    pl.when(later)(arrival(hop_1, hop_sem.at[0], first, face).wait_recv)
    send(later, hop_1, hop_2, hop_sem.at[1], partner, face)
    for f in range(2):
        send(not_top, fields.at[f, CZ - 1], zh.at[0, f], z_sem.at[0, f], above, face)
        send(not_bottom, fields.at[f, 0], zh.at[1, f], z_sem.at[1, f], below, face)
    meanwhile()
    for side, condition in ((0, has_left), (1, has_right)):
        for f in range(2):
            pl.when(condition)(
                arrival(xh.at[side, f, pl.ds(1, CZ)], edge_sem.at[side, f], partner, face).wait_recv
            )
            send(both(condition, not_top), xh.at[side, f, CZ], xh.at[side, f, 0], corner_sem.at[side, f, 0], above, face)
            send(both(condition, not_bottom), xh.at[side, f, 1], xh.at[side, f, CZ + 1], corner_sem.at[side, f, 1], below, face)
    arrival(hop_2, hop_sem.at[1], partner, face).wait_recv()
    f, x = y_chip // 4, lax.rem(y_chip, 4)
    side = 1 - core
    plane = 3 * side
    send(None, hop_2, zh.at[side, f, x, rows(x_chip), :], z_sem.at[side, f], last, face)
    for to, condition, peer in (
        (0, both(sends_right, has_right), face + 1),
        (1, both(sends_left, has_left), face - 1),
    ):
        send(condition, hop_2, xh.at[to, f, plane, rows(x_chip), :], corner_sem.at[to, f, side], last, peer)

    def wait_side(end):
        for f in range(2):
            arrival(zh.at[end, f], z_sem.at[end, f], partner, face).wait_recv()

        def wait_corners(side):
            for f in range(2):
                arrival(xh.at[side, f, 3 * end], corner_sem.at[side, f, end], partner, face).wait_recv()

        pl.when(has_left)(functools.partial(wait_corners, 0))
        pl.when(has_right)(functools.partial(wait_corners, 1))

    def clear(side):
        xh[side] = jnp.zeros_like(xh[side])

    pl.when(jnp.logical_not(has_left))(functools.partial(clear, 0))
    pl.when(jnp.logical_not(has_right))(functools.partial(clear, 1))

    def finish():
        for condition, copy in started:
            if condition is None:
                copy.wait_send()
            else:
                pl.when(condition)(copy.wait_send)

    return wait_side, finish


def forecast_kernel(
    fields, mask_in, chosen_in, kernel_in, bias_in, read_in, cells_in, values_in, sigma_in,
    sat_hbm, total_out,
    sat_out, fields_here, mask, chosen, kernel_t, bias, read, cells, values, sigma, load_sem,
    padded_0, padded_1, rows_0, rows_1, weights, sat_0, sat_1, predicted, part,
    zh, xh, hop_1, hop_2, sent, z_sem, edge_sem, corner_sem, hop_sem, *total_scratch,
):
    loads = [
        pltpu.make_async_copy(src, dst, load_sem.at[n])
        for n, (src, dst) in enumerate(
            (
                (fields, fields_here), (mask_in, mask), (chosen_in, chosen), (kernel_in, kernel_t),
                (bias_in, bias), (read_in, read), (cells_in, cells), (values_in, values),
                (sigma_in, sigma),
            )
        )
    ]
    for load in loads:
        load.start()

    def place(row, block):
        block = block.astype(F32)
        own = pl.ds(pl.multiple_of(row * PITCH + HEAD, 8), CY)
        padded_0[own, :] = block[:, 0:128]
        padded_1[own, :] = block[:, 128:256]

    def slot(f, z, x):
        return (2 * z + f) * (CX + 2) + x

    def prepare():
        for load in loads:
            load.wait()
        own_rows()
        make_weights()

    def own_rows():
        blank = jnp.zeros((8, 128), F32)
        for row in range(ROWS):
            for padded in (padded_0, padded_1):
                padded[pl.ds(row * PITCH, 8), :] = blank
                padded[pl.ds(row * PITCH + HEAD + CY, 8), :] = blank
        for padded in (padded_0, padded_1):
            padded[ROWS * PITCH :, :] = jnp.zeros((4 * PITCH, 128), F32)
        for f in range(2):
            for x in range(CX):
                for z in range(CZ):
                    place(slot(f, z + 1, x + 1), fields_here[f, z, x])

    def make_weights():
        taps = kernel_t[...]
        for out in range(OUTS):
            piece = jnp.dot(taps, chosen[out], preferred_element_type=F32)
            rows_0[pl.ds(out * CH, CH), :] = piece[:, 0:128]
            rows_1[pl.ds(out * CH, CH), :] = piece[:, 128:256]
        lane = lax.broadcasted_iota(jnp.int32, (OUTS, 16), 1)
        for c in range(CH):
            own = pl.ds(c * OUTS, OUTS)
            every = pl.ds(c, OUTS, stride=CH)
            weights[own, 0:128] = (rows_0[every, :] * 0.5).astype(BF16)
            weights[own, 128:256] = (rows_1[every, :] * 0.5).astype(BF16)
            whole = jnp.full((OUTS, 16), bias[c] * 0.5, F32)
            high = whole.astype(BF16).astype(F32)
            middle = (whole - high).astype(BF16).astype(F32)
            low = whole - high - middle
            split = jnp.where(
                lane == 0, high, jnp.where(lane == 1, middle, jnp.where(lane == 2, low, 0.0))
            )
            weights[own, DEPTH : DEPTH + 16] = split.astype(BF16)

    greet_total, sum_over_devices = total(part, total_out, *total_scratch)
    wait_side, finish = exchange(
        fields, zh, xh, hop_1, hop_2, sent, z_sem, edge_sem, corner_sem, hop_sem,
        greet_total, PEERS, prepare,
    )

    def place_side(end):
        for f in range(2):
            for x in range(CX):
                place(slot(f, 3 * end, x + 1), zh[end, f, x])
            place(slot(f, 3 * end, 0), xh[0, f, 3 * end])
            place(slot(f, 3 * end, CX + 1), xh[1, f, 3 * end])

    ones = jnp.ones((256 - DEPTH, 128), F32)

    def step(plane, t, carry):
        halves = []
        start = plane * (2 * (CX + 2) * PITCH) + HEAD - 1 + 4 * t
        for padded in (padded_0, padded_1):
            rows = [padded[pl.ds(start + q, SPAN, stride=PITCH), :] for q in range(6)]
            halves.append(jnp.concatenate(rows + [ones], axis=0).astype(BF16))
        inputs = jnp.concatenate(halves, axis=1)
        half = jnp.dot(weights[...], inputs, preferred_element_type=F32)
        total = jnp.zeros((OUTS, MEM), F32)
        for c in range(CH):
            h = half[c * OUTS : (c + 1) * OUTS]
            total = total + read[c] * (h + h * jnp.tanh(h))
        level = 0.5 + 0.5 * jnp.tanh(0.5 * total)
        for yo in range(4):
            cells_of = pl.ds(plane * (CX * CY) + 4 * t + yo, CX, stride=CY)
            sat_0[cells_of, :] = level[yo * CX : yo * CX + CX, 0:128]
            sat_1[cells_of, :] = level[yo * CX : yo * CX + CX, 128:256]
        return carry

    core = lax.rem(lax.axis_index("cores"), 2)
    for f in range(2):
        for z in range(1, CZ + 1):
            place(slot(f, z, 0), xh[0, f, z])
            place(slot(f, z, CX + 1), xh[1, f, z])
    for plane in (1 - core, core):
        wait_side(plane)
        place_side(plane)
        lax.fori_loop(0, CY // 4, functools.partial(step, plane), 0, unroll=8)

    columns = jnp.concatenate([mask[0], mask[1]], axis=0).astype(F32).T
    for zx in range(CZ * CX):
        own = pl.ds(zx * CY, CY)
        for lane_0, sat in ((0, sat_0), (128, sat_1)):
            rounded = (sat[own, :] * columns[:, zx : zx + 1]).astype(BF16)
            sat_out[own, lane_0 : lane_0 + 128] = rounded
            sat[own, :] = rounded.astype(F32)

    store = pltpu.make_async_copy(sat_out, sat_hbm, load_sem.at[9])
    store.start()

    for o in range(OBS):
        predicted[pl.ds(o, 1), 0:128] = sat_0[pl.ds(cells[o], 1), :]
        predicted[pl.ds(o, 1), 128:256] = sat_1[pl.ds(cells[o], 1), :]
    diagonal = lax.broadcasted_iota(jnp.int32, (OBS, OBS), 0) == lax.broadcasted_iota(
        jnp.int32, (OBS, OBS), 1
    )

    def column(row):
        return jnp.sum(jnp.where(diagonal, row[...], 0.0), axis=1, keepdims=True)

    inverse_sigma = 1.0 / column(sigma)
    pred = predicted[...]
    center = jnp.sum(pred, axis=1, keepdims=True) * (1.0 / MEM)
    scaled = (pred - center) * (inverse_sigma * (1.0 / ROOT))
    innovation = (column(values) - center) * inverse_sigma
    gram = lax.dot_general(
        scaled, scaled, (((0,), (0,)), ((), ())), precision=HIGHEST, preferred_element_type=F32
    )
    coeff = jnp.sum(scaled * innovation, axis=0, keepdims=True) * (1.0 / ROOT)
    part[0:MEM, :] = gram[:, 0:128]
    part[MEM : 2 * MEM, :] = gram[:, 128:256]
    part[MEM : MEM + 1, :] = coeff[:, 0:128]
    part[MEM + 1 : MEM + 2, :] = coeff[:, 128:256]
    sum_over_devices()
    finish()
    store.wait()


def forecast(fields, mask, kernel, bias, read, cells, values, sigma):
    chosen = jnp.asarray(tap_selection(), BF16)
    dma = pltpu.SemaphoreType.DMA
    return pl.pallas_call(
        forecast_kernel,
        out_shape=(
            jax.ShapeDtypeStruct((CELLS, MEM), BF16),
            jax.ShapeDtypeStruct((2 * MEM, 128), F32),
        ),
        in_specs=[pl.BlockSpec(memory_space=pltpu.HBM)] * 9,
        out_specs=(pl.BlockSpec(memory_space=pltpu.HBM), VMEM),
        scratch_shapes=[
            pltpu.VMEM((CELLS, MEM), BF16),
            pltpu.VMEM((2, CZ, CX, CY, MEM), BF16),
            pltpu.VMEM((CZ, CX, CY), jnp.int32),
            pltpu.VMEM((OUTS, TAPS, 256), BF16),
            pltpu.VMEM((CH, TAPS), BF16),
            pltpu.SMEM((CH,), F32),
            pltpu.SMEM((CH,), F32),
            pltpu.SMEM((OBS,), jnp.int32),
            pltpu.VMEM((1, OBS), F32),
            pltpu.VMEM((1, OBS), F32),
            dma((10,)),
            pltpu.VMEM(((ROWS + 4) * PITCH, 128), F32),
            pltpu.VMEM(((ROWS + 4) * PITCH, 128), F32),
            pltpu.VMEM((OUTS * CH, 128), F32),
            pltpu.VMEM((OUTS * CH, 128), F32),
            pltpu.VMEM((OUTS * CH, 256), BF16),
            pltpu.VMEM((CELLS, 128), F32),
            pltpu.VMEM((CELLS, 128), F32),
            pltpu.VMEM((OBS, MEM), F32),
            pltpu.VMEM((2 * MEM, 128), F32),
            pltpu.VMEM((2, 2, 4, CY, MEM), BF16),
            pltpu.VMEM((2, 2, 4, CY, MEM), BF16),
            pltpu.VMEM((CY // 4, MEM), BF16),
            pltpu.VMEM((CY // 4, MEM), BF16),
            dma((56,)),
            dma((2, 2)),
            dma((2, 2)),
            dma((2, 2, 2)),
            dma((2,)),
            pltpu.VMEM((8, 64, 128), F32),
            pltpu.VMEM((8, 8, 128), F32),
            pltpu.VMEM((16, 8, 128), F32),
            pltpu.VMEM((64, 128), F32),
            pltpu.VMEM((8, 128), F32),
            pltpu.VMEM((64, 128), F32),
        ]
        + [dma((n,)) for n in (8, 8, 8, 8, 16, 16, 8, 8, 8, 8)],
        compiler_params=pltpu.CompilerParams(
            collective_id=1, has_side_effects=True, vmem_limit_bytes=63 << 20
        ),
        name="forecast",
    )(
        fields, mask, chosen, kernel.T, bias, read, cells,
        values.reshape(1, OBS), sigma.reshape(1, OBS),
    )


def total(
    part, out, from_a, from_b, from_c, sum_a, sum_b, whole,
    send_a, recv_a, send_b, recv_b, send_c, recv_c, send_d, recv_d, send_e, recv_e,
):
    cores = lax.axis_index("cores")
    face = lax.axis_index("face")
    a = lax.rem(cores, 8)
    y = lax.rem(cores // 8, 8)
    high = cores // 64
    z = high * 8 + face

    def peer_a(d):
        return (cores - a + lax.rem(a + d, 8), face)

    def peer_b(d):
        return (high * 64 + lax.rem(y + d, 8) * 8 + a, face)

    def peer_c(d):
        other = lax.rem(z + d, 16)
        return (other // 8 * 64 + lax.rem(cores, 64), lax.rem(other, 8))

    def greet(barrier):
        for d in range(1, 8):
            pl.semaphore_signal(barrier, inc=1, device_id=peer_a(d), device_id_type=MESH)
            pl.semaphore_signal(barrier, inc=1, device_id=peer_b(d), device_id_type=MESH)
        for d in range(1, 16):
            pl.semaphore_signal(barrier, inc=1, device_id=peer_c(d), device_id_type=MESH)

    def sum_over_devices():
        def send(src, dst, sems, d, peer):
            copy = pltpu.make_async_remote_copy(
                src_ref=src, dst_ref=dst, send_sem=sems[0].at[d], recv_sem=sems[1].at[d],
                device_id=peer, device_id_type=MESH,
            )
            copy.start()
            return copy

        def rows(index, size):
            return pl.ds(pl.multiple_of(index * size, size), size)

        copies = []

        def stage(make, count):
            started = [make(d) for d in range(1, count)]
            copies.extend(started)
            return started

        for copy in stage(
            lambda d: send(part.at[rows(lax.rem(a + d, 8), 64), :], from_a.at[d], (send_a, recv_a), d, peer_a(d)), 8
        ):
            pass
        started = copies[-7:]
        value = part[rows(a, 64), :]
        for d in range(1, 8):
            started[d - 1].wait_recv()
            value = value + from_a[d]
        sum_a[...] = value
        started = stage(
            lambda d: send(sum_a.at[rows(lax.rem(y + d, 8), 8), :], from_b.at[d], (send_b, recv_b), d, peer_b(d)), 8
        )
        value = sum_a[rows(y, 8), :]
        for d in range(1, 8):
            started[d - 1].wait_recv()
            value = value + from_b[d]
        sum_b[...] = value
        started = stage(lambda d: send(sum_b, from_c.at[d], (send_c, recv_c), d, peer_c(d)), 16)
        for d in range(1, 16):
            started[d - 1].wait_recv()
            value = value + from_c[d]
        mine = whole.at[rows(y, 8), :]
        mine[...] = value
        started = stage(lambda d: send(mine, mine, (send_d, recv_d), d, peer_b(d)), 8)
        for d in range(1, 8):
            started[d - 1].wait_recv()
        place = out.at[rows(a, 64), :]
        started = stage(lambda d: send(whole, place, (send_e, recv_e), d, peer_a(d)), 8)
        place[...] = whole[...]
        for d in range(1, 8):
            started[d - 1].wait_recv()
        for copy in copies:
            copy.wait_send()

    return greet, sum_over_devices


PEERS = 7 + 7 + 15


BLOCK = 128


def analysis_kernel(
    gram_hbm, fields_hbm, sat_hbm, out_hbm,
    gram_in, fields, sat, out, gram, inverse, load_sem, store_sem,
):
    loads = [
        pltpu.make_async_copy(src, dst, load_sem.at[n])
        for n, (src, dst) in enumerate(((gram_hbm, gram_in), (fields_hbm, fields), (sat_hbm, sat)))
    ]
    for load in loads:
        load.start()
    loads[0].wait()
    row_index = lax.broadcasted_iota(jnp.int32, (MEM, MEM), 0)
    column_index = lax.broadcasted_iota(jnp.int32, (MEM, MEM), 1)
    identity = jnp.where(row_index == column_index, 1.0, 0.0)
    gram[:, 0:128] = gram_in[0:MEM, :]
    gram[:, 128:256] = gram_in[MEM : 2 * MEM, :]
    coeff = jnp.concatenate(
        [gram_in[MEM : MEM + 1, :], gram_in[MEM + 1 : MEM + 2, :]], axis=1
    )
    gram[0:128, 128:256] = gram_in[128:256, :].T
    gram[...] = gram[...] + identity
    inverse[...] = identity

    small_row = lax.broadcasted_iota(jnp.int32, (BLOCK, 2 * BLOCK), 0)
    small_column = lax.broadcasted_iota(jnp.int32, (BLOCK, 2 * BLOCK), 1)
    odd = lax.rem(small_row[:, 0:1], 2) == 1
    corner = jnp.where(small_row + BLOCK == small_column, 1.0, 0.0)[:, BLOCK:]
    both = (((0,), (0,)), ((), ()))

    def product(left, right):
        return jnp.dot(left, right, precision=HIGHEST, preferred_element_type=F32)

    def wide(column):
        return jnp.broadcast_to(column, (column.shape[0], 2 * BLOCK))

    def down(block):
        return jnp.concatenate([block[-1:], block[:-1]], axis=0)

    for k in range(0, MEM, BLOCK):
        after = k + BLOCK
        work = jnp.concatenate([gram[k:after, k:after], corner], axis=1)
        finished = []
        for i in range(0, BLOCK, 4):
            if i and i % 8 == 0:
                finished.append(work[:8])
                work = work[8:]
            row = i % 8
            r0, r1, r2, r3 = (work[row + q : row + q + 1, :] for q in range(4))
            at = [slice(i + q, i + q + 1) for q in range(4)]
            a00, a01, a02, a03 = (wide(r0[:, at[q]]) for q in range(4))
            a11, a12, a13 = (wide(r1[:, at[q]]) for q in range(1, 4))
            a22, a23, a33 = wide(r2[:, at[2]]), wide(r2[:, at[3]]), wide(r3[:, at[3]])
            c0, c1, c2, c3 = (wide(work[:, at[q]]) for q in range(4))
            inverse_det = 1.0 / (a00 * a11 - a01 * a01)
            p00, p01, p11 = a11 * inverse_det, -a01 * inverse_det, a00 * inverse_det
            x02, x12 = p00 * a02 + p01 * a12, p01 * a02 + p11 * a12
            x03, x13 = p00 * a03 + p01 * a13, p01 * a03 + p11 * a13
            b22 = a22 - (a02 * x02 + a12 * x12)
            b23 = a23 - (a02 * x03 + a12 * x13)
            b33 = a33 - (a03 * x03 + a13 * x13)
            inverse_det = 1.0 / (b22 * b33 - b23 * b23)
            q22, q23, q33 = b33 * inverse_det, -b23 * inverse_det, b22 * inverse_det
            s0, s1 = p00 * r0 + p01 * r1, p01 * r0 + p11 * r1
            r2 = r2 - (a02 * s0 + a12 * s1)
            r3 = r3 - (a03 * s0 + a13 * s1)
            s2, s3 = q22 * r2 + q23 * r3, q23 * r2 + q33 * r3
            c2 = c2 - (c0 * x02 + c1 * x12)
            c3 = c3 - (c0 * x03 + c1 * x13)
            first = small_row[: work.shape[0]] > row + 1
            second = small_row[: work.shape[0]] > row + 3
            work = work - (
                (jnp.where(first, c0, 0.0) * s0 + jnp.where(first, c1, 0.0) * s1)
                + (jnp.where(second, c2, 0.0) * s2 + jnp.where(second, c3, 0.0) * s3)
            )
        work = jnp.concatenate(finished + [work], axis=0)
        diagonal = jnp.sum(jnp.where(small_row == small_column, work, 0.0), axis=1, keepdims=True)
        beside = jnp.sum(
            jnp.where(small_row - 1 == small_column, work, 0.0), axis=1, keepdims=True
        )
        ratio = jnp.where(odd, beside / down(diagonal), 0.0)
        pivots = diagonal - ratio * beside
        right = work[:, BLOCK:]
        lower = (right - ratio * down(right)) * (1.0 / jnp.sqrt(pivots))
        inverse_rows = product(lower, inverse[k:after, :])
        inverse[k:after, :] = inverse_rows
        if after < MEM:
            upper_rows = product(lower, gram[k:after, :])
            turned = upper_rows[:, after:]
            gram[after:, :] = gram[after:, :] - lax.dot_general(
                turned, upper_rows, both, precision=HIGHEST, preferred_element_type=F32
            )
            inverse[after:, :] = inverse[after:, :] - lax.dot_general(
                turned, inverse_rows, both, precision=HIGHEST, preferred_element_type=F32
            )

    low = jnp.where(row_index >= column_index, inverse[...], 0.0)
    half_way = jnp.sum(low * coeff, axis=1, keepdims=True)
    weights = jnp.sum(low * half_way, axis=0, keepdims=True)
    mixing_t = (low + weights).astype(BF16)

    def update(state):
        state = state.astype(F32)
        mean = jnp.sum(state, axis=1, keepdims=True) * (1.0 / MEM)
        moved = lax.dot_general(
            (state - mean).astype(BF16), mixing_t, (((1,), (1,)), ((), ())),
            preferred_element_type=F32,
        )
        return (mean + moved).astype(BF16)

    loads[1].wait()
    loads[2].wait()
    stores = []
    for z in range(CZ):
        for x in range(CX):
            for f in range(3):
                out[f, z, x] = update(fields[f, z, x] if f < 2 else sat[z, x])
            store = pltpu.make_async_copy(
                out.at[:, z, x], out_hbm.at[:, z, x], store_sem.at[z * CX + x]
            )
            store.start()
            stores.append(store)
    for store in stores:
        store.wait()


def analysis(gram, fields, sat):
    return pl.pallas_call(
        analysis_kernel,
        out_shape=jax.ShapeDtypeStruct((3,) + fields.shape[1:], BF16),
        in_specs=[pl.BlockSpec(memory_space=pltpu.HBM)] * 3,
        out_specs=pl.BlockSpec(memory_space=pltpu.HBM),
        scratch_shapes=[
            pltpu.VMEM(gram.shape, F32),
            pltpu.VMEM(fields.shape, BF16),
            pltpu.VMEM(sat.shape, BF16),
            pltpu.VMEM((3,) + fields.shape[1:], BF16),
            pltpu.VMEM((MEM, MEM), F32),
            pltpu.VMEM((MEM, MEM), F32),
            pltpu.SemaphoreType.DMA((3,)),
            pltpu.SemaphoreType.DMA((CZ * CX,)),
        ],
        compiler_params=pltpu.CompilerParams(vmem_limit_bytes=63 << 20),
        name="analysis",
    )(gram, fields, sat)


def shards(
    fields, pore_mask, conv_kernel, conv_bias, read_weight, obs_cells, obs_values, obs_sigma
):
    sat, summed = forecast(
        fields, pore_mask, conv_kernel, conv_bias, read_weight, obs_cells, obs_values, obs_sigma
    )
    return analysis(summed, fields, sat.reshape(CZ, CX, CY, MEM))


def solution(mesh):
    return jax.shard_map(
        shards,
        mesh=mesh,
        in_specs=(
            P(None, "cores", "face", None, None),
            P("cores", "face", None),
            P(),
            P(),
            P(),
            P(("cores", "face")),
            P(("cores", "face")),
            P(("cores", "face")),
        ),
        out_specs=P(None, "cores", "face", None, None),
        check_vma=False,
    )
```

```python
import functools
import math

import jax
import jax.numpy as jnp
import numpy as np
from jax import lax
from jax.experimental import pallas as pl
from jax.experimental.pallas import tpu as pltpu
from jax.sharding import PartitionSpec as P

MESH = pl.DeviceIdType.MESH
HIGHEST = lax.Precision.HIGHEST
F32 = jnp.float32
BF16 = jnp.bfloat16
VMEM = pl.BlockSpec(memory_space=pltpu.VMEM)
SMEM = pl.BlockSpec(memory_space=pltpu.SMEM)

CH = 32
CZ, CX, CY, MEM = 2, 4, 128, 256
CELLS = CZ * CX * CY
OBS = 64
TAPS = 54
ROWS = 2 * (CZ + 2) * (CX + 2)
SPAN = 40
PITCH = 144
HEAD = 8
OUTS = 4 * CX
DEPTH = 6 * SPAN
ROOT = math.sqrt(MEM - 1)
HALF = MEM // 2
TILES = 5
SUMMED = 8 * 8 * TILES


def tap_selection():
    chosen = np.zeros((OUTS, TAPS, 256), np.float32)
    for yo in range(4):
        for xo in range(CX):
            for f in range(2):
                for a in range(3):
                    for b in range(3):
                        for c in range(3):
                            row = (2 * a + f) * (CX + 2) + xo + b
                            chosen[
                                yo * CX + xo, 27 * f + 9 * a + 3 * b + c, (yo + c) * SPAN + row
                            ] = 1.0
    return chosen


def exchange(
    fields, zh, xh, hop_1, hop_2, sent, z_sem, edge_sem, corner_sem, hop_sem, greet_more, more, meanwhile
):
    cores = lax.axis_index("cores")
    face = lax.axis_index("face")
    core = lax.rem(cores, 2)
    x_chip = lax.rem(cores // 2, 4)
    y_chip = lax.rem(cores // 8, 8)
    high = cores // 64
    above, below = lax.rem(cores + 1, 128), lax.rem(cores + 127, 128)
    top, bottom = lax.rem(cores, 64) == 63, lax.rem(cores, 64) == 0
    not_top, not_bottom = jnp.logical_not(top), jnp.logical_not(bottom)
    has_left, has_right = face > 0, face < 7
    partner = lax.rem(cores + 64, 128)
    first = high * 64 + core * 63
    last = high * 64 + 63 - core * 63
    is_first = cores == first
    later = jnp.logical_not(is_first)
    sends_right = lax.rem(y_chip, 4) == 3
    sends_left = lax.rem(y_chip, 4) == 0

    def both(*conditions):
        return functools.reduce(jnp.logical_and, conditions)

    barrier = pltpu.get_barrier_semaphore()

    def greet(condition, *peers):
        def signal():
            for peer in peers:
                pl.semaphore_signal(barrier, inc=1, device_id=peer, device_id_type=MESH)

        if condition is None:
            signal()
        else:
            pl.when(condition)(signal)

    def columns(core_of, rows, face_of):
        return [(high * 64 + j * 8 + i * 2 + core_of, face_of) for j in rows for i in range(4)]

    greet_more(barrier)
    greet(None, (partner, face))
    greet(later, (first, face))
    greet(not_bottom, (below, face))
    greet(not_top, (above, face))
    greet(has_left, (cores, face - 1))
    greet(has_right, (cores, face + 1))
    for end, core_of in ((bottom, 1), (top, 0)):
        greet(end, *columns(core_of, range(8), face))
        greet(both(end, has_left), *columns(core_of, (3, 7), face - 1))
        greet(both(end, has_right), *columns(core_of, (0, 4), face + 1))

    def one(condition):
        return jnp.where(condition, 1, 0)

    expected = (
        2
        + more
        + one(not_top)
        + one(not_bottom)
        + one(has_left)
        + one(has_right)
        + one(both(sends_right, has_right))
        + one(both(sends_left, has_left))
        + 31 * one(is_first)
    )
    pl.semaphore_wait(barrier, expected)

    started = []

    def send(condition, src, dst, arrived, *peer):
        copy = pltpu.make_async_remote_copy(
            src_ref=src, dst_ref=dst, send_sem=sent.at[len(started)], recv_sem=arrived,
            device_id=peer, device_id_type=MESH,
        )
        started.append((condition, copy))
        if condition is None:
            copy.start()
        else:
            pl.when(condition)(copy.start)

    def arrival(dst, arrived, *peer):
        return pltpu.make_async_remote_copy(
            src_ref=dst, dst_ref=dst, send_sem=sent.at[0], recv_sem=arrived,
            device_id=peer, device_id_type=MESH,
        )

    part = CY // 4

    def rows(quarter):
        return pl.ds(pl.multiple_of(quarter * part, part), part)

    def piece(j, i):
        return fields.at[j // 4, core, lax.rem(j, 4), rows(i), :]

    for n in range(31):
        at = n + 1 - core
        j, i = at // 4, lax.rem(at, 4)
        send(is_first, piece(j, i), hop_1, hop_sem.at[0], high * 64 + at * 2 + core, face)
    send(is_first, piece(y_chip, x_chip), hop_2, hop_sem.at[1], partner, face)
    for side, x, condition, peer in (
        (0, CX - 1, has_right, face + 1),
        (1, 0, has_left, face - 1),
    ):
        for f in range(2):
            send(condition, fields.at[f, :, x], xh.at[side, f, pl.ds(1, CZ)], edge_sem.at[side, f], cores, peer)
    pl.when(later)(arrival(hop_1, hop_sem.at[0], first, face).wait_recv)
    send(later, hop_1, hop_2, hop_sem.at[1], partner, face)
    for f in range(2):
        send(not_top, fields.at[f, CZ - 1], zh.at[0, f], z_sem.at[0, f], above, face)
        send(not_bottom, fields.at[f, 0], zh.at[1, f], z_sem.at[1, f], below, face)
    meanwhile()
    for side, condition in ((0, has_left), (1, has_right)):
        for f in range(2):
            pl.when(condition)(
                arrival(xh.at[side, f, pl.ds(1, CZ)], edge_sem.at[side, f], partner, face).wait_recv
            )
            send(both(condition, not_top), xh.at[side, f, CZ], xh.at[side, f, 0], corner_sem.at[side, f, 0], above, face)
            send(both(condition, not_bottom), xh.at[side, f, 1], xh.at[side, f, CZ + 1], corner_sem.at[side, f, 1], below, face)
    arrival(hop_2, hop_sem.at[1], partner, face).wait_recv()
    f, x = y_chip // 4, lax.rem(y_chip, 4)
    side = 1 - core
    plane = 3 * side
    send(None, hop_2, zh.at[side, f, x, rows(x_chip), :], z_sem.at[side, f], last, face)
    for to, condition, peer in (
        (0, both(sends_right, has_right), face + 1),
        (1, both(sends_left, has_left), face - 1),
    ):
        send(condition, hop_2, xh.at[to, f, plane, rows(x_chip), :], corner_sem.at[to, f, side], last, peer)

    def wait_side(end):
        for f in range(2):
            arrival(zh.at[end, f], z_sem.at[end, f], partner, face).wait_recv()

        def wait_corners(side):
            for f in range(2):
                arrival(xh.at[side, f, 3 * end], corner_sem.at[side, f, end], partner, face).wait_recv()

        pl.when(has_left)(functools.partial(wait_corners, 0))
        pl.when(has_right)(functools.partial(wait_corners, 1))

    def clear(side):
        xh[side] = jnp.zeros_like(xh[side])

    pl.when(jnp.logical_not(has_left))(functools.partial(clear, 0))
    pl.when(jnp.logical_not(has_right))(functools.partial(clear, 1))

    def finish():
        for condition, copy in started:
            if condition is None:
                copy.wait_send()
            else:
                pl.when(condition)(copy.wait_send)

    return wait_side, finish


def half_indices():
    shape = (HALF, HALF)
    return lax.broadcasted_iota(jnp.int32, shape, 0), lax.broadcasted_iota(jnp.int32, shape, 1)


def packed(gram, coeff):
    row, column = half_indices()
    last = gram[HALF:, HALF:]
    diagonal = jnp.sum(jnp.where(row == column, last, 0.0), axis=0, keepdims=True)
    return jnp.concatenate(
        [
            gram[HALF:, :HALF],
            jnp.where(row >= column, gram[:HALF, :HALF], last),
            diagonal,
            coeff[:, :HALF],
            coeff[:, HALF:],
            jnp.zeros((SUMMED - MEM - 3, HALF), F32),
        ],
        axis=0,
    )


def unpacked(rows):
    row, column = half_indices()
    corner = rows[:HALF]
    joint = rows[HALF:MEM]
    turned = joint.T
    first = jnp.where(row >= column, joint, turned)
    last = jnp.where(row == column, rows[MEM : MEM + 1], jnp.where(row < column, joint, turned))
    coeff = jnp.concatenate([rows[MEM + 1 : MEM + 2], rows[MEM + 2 : MEM + 3]], axis=1)
    return first, corner, last, coeff


def forecast_kernel(
    fields, mask_in, chosen_in, kernel_in, bias_in, read_in, cells_in, values_in, sigma_in,
    sat_hbm, total_out,
    sat_out, fields_here, mask, chosen, kernel_t, bias, read, cells, values, sigma, load_sem,
    padded_0, padded_1, rows_0, rows_1, weights, sat_0, sat_1, predicted, part,
    zh, xh, hop_1, hop_2, sent, z_sem, edge_sem, corner_sem, hop_sem, *total_scratch,
):
    loads = [
        pltpu.make_async_copy(src, dst, load_sem.at[n])
        for n, (src, dst) in enumerate(
            (
                (fields, fields_here), (mask_in, mask), (chosen_in, chosen), (kernel_in, kernel_t),
                (bias_in, bias), (read_in, read), (cells_in, cells), (values_in, values),
                (sigma_in, sigma),
            )
        )
    ]
    for load in loads:
        load.start()

    def place(row, block):
        block = block.astype(F32)
        own = pl.ds(pl.multiple_of(row * PITCH + HEAD, 8), CY)
        padded_0[own, :] = block[:, 0:128]
        padded_1[own, :] = block[:, 128:256]

    def slot(f, z, x):
        return (2 * z + f) * (CX + 2) + x

    def prepare():
        for load in loads:
            load.wait()
        own_rows()
        make_weights()

    def own_rows():
        blank = jnp.zeros((8, 128), F32)
        for row in range(ROWS):
            for padded in (padded_0, padded_1):
                padded[pl.ds(row * PITCH, 8), :] = blank
                padded[pl.ds(row * PITCH + HEAD + CY, 8), :] = blank
        for padded in (padded_0, padded_1):
            padded[ROWS * PITCH :, :] = jnp.zeros((4 * PITCH, 128), F32)
        for f in range(2):
            for x in range(CX):
                for z in range(CZ):
                    place(slot(f, z + 1, x + 1), fields_here[f, z, x])

    def make_weights():
        taps = kernel_t[...]
        for out in range(OUTS):
            piece = jnp.dot(taps, chosen[out], preferred_element_type=F32)
            rows_0[pl.ds(out * CH, CH), :] = piece[:, 0:128]
            rows_1[pl.ds(out * CH, CH), :] = piece[:, 128:256]
        lane = lax.broadcasted_iota(jnp.int32, (OUTS, 16), 1)
        for c in range(CH):
            own = pl.ds(c * OUTS, OUTS)
            every = pl.ds(c, OUTS, stride=CH)
            weights[own, 0:128] = (rows_0[every, :] * 0.5).astype(BF16)
            weights[own, 128:256] = (rows_1[every, :] * 0.5).astype(BF16)
            whole = jnp.full((OUTS, 16), bias[c] * 0.5, F32)
            high = whole.astype(BF16).astype(F32)
            middle = (whole - high).astype(BF16).astype(F32)
            low = whole - high - middle
            split = jnp.where(
                lane == 0, high, jnp.where(lane == 1, middle, jnp.where(lane == 2, low, 0.0))
            )
            weights[own, DEPTH : DEPTH + 16] = split.astype(BF16)

    greet_total, sum_over_devices = total(part, total_out, *total_scratch)
    wait_side, finish = exchange(
        fields, zh, xh, hop_1, hop_2, sent, z_sem, edge_sem, corner_sem, hop_sem,
        greet_total, PEERS, prepare,
    )

    def place_side(end):
        for f in range(2):
            for x in range(CX):
                place(slot(f, 3 * end, x + 1), zh[end, f, x])
            place(slot(f, 3 * end, 0), xh[0, f, 3 * end])
            place(slot(f, 3 * end, CX + 1), xh[1, f, 3 * end])

    ones = jnp.ones((256 - DEPTH, 128), F32)

    def step(plane, t, carry):
        halves = []
        start = plane * (2 * (CX + 2) * PITCH) + HEAD - 1 + 4 * t
        for padded in (padded_0, padded_1):
            rows = [padded[pl.ds(start + q, SPAN, stride=PITCH), :] for q in range(6)]
            halves.append(jnp.concatenate(rows + [ones], axis=0).astype(BF16))
        inputs = jnp.concatenate(halves, axis=1)
        half = jnp.dot(weights[...], inputs, preferred_element_type=F32)
        total = jnp.zeros((OUTS, MEM), F32)
        for c in range(CH):
            h = half[c * OUTS : (c + 1) * OUTS]
            total = total + read[c] * (h + h * jnp.tanh(h))
        level = 0.5 + 0.5 * jnp.tanh(0.5 * total)
        for yo in range(4):
            cells_of = pl.ds(plane * (CX * CY) + 4 * t + yo, CX, stride=CY)
            sat_0[cells_of, :] = level[yo * CX : yo * CX + CX, 0:128]
            sat_1[cells_of, :] = level[yo * CX : yo * CX + CX, 128:256]
        return carry

    core = lax.rem(lax.axis_index("cores"), 2)
    for f in range(2):
        for z in range(1, CZ + 1):
            place(slot(f, z, 0), xh[0, f, z])
            place(slot(f, z, CX + 1), xh[1, f, z])
    for plane in (1 - core, core):
        wait_side(plane)
        place_side(plane)
        lax.fori_loop(0, CY // 4, functools.partial(step, plane), 0, unroll=8)

    columns = jnp.concatenate([mask[0], mask[1]], axis=0).astype(F32).T
    for zx in range(CZ * CX):
        own = pl.ds(zx * CY, CY)
        for lane_0, sat in ((0, sat_0), (128, sat_1)):
            rounded = (sat[own, :] * columns[:, zx : zx + 1]).astype(BF16)
            sat_out[own, lane_0 : lane_0 + 128] = rounded
            sat[own, :] = rounded.astype(F32)

    store = pltpu.make_async_copy(sat_out, sat_hbm, load_sem.at[9])
    store.start()

    for o in range(OBS):
        predicted[pl.ds(o, 1), 0:128] = sat_0[pl.ds(cells[o], 1), :]
        predicted[pl.ds(o, 1), 128:256] = sat_1[pl.ds(cells[o], 1), :]
    diagonal = lax.broadcasted_iota(jnp.int32, (OBS, OBS), 0) == lax.broadcasted_iota(
        jnp.int32, (OBS, OBS), 1
    )

    def column(row):
        return jnp.sum(jnp.where(diagonal, row[...], 0.0), axis=1, keepdims=True)

    inverse_sigma = 1.0 / column(sigma)
    pred = predicted[...]
    center = jnp.sum(pred, axis=1, keepdims=True) * (1.0 / MEM)
    scaled = (pred - center) * (inverse_sigma * (1.0 / ROOT))
    innovation = (column(values) - center) * inverse_sigma
    gram = lax.dot_general(
        scaled, scaled, (((0,), (0,)), ((), ())), precision=HIGHEST, preferred_element_type=F32
    )
    coeff = jnp.sum(scaled * innovation, axis=0, keepdims=True) * (1.0 / ROOT)
    part[...] = packed(gram, coeff)
    sum_over_devices()
    finish()
    store.wait()


def forecast(fields, mask, kernel, bias, read, cells, values, sigma):
    chosen = jnp.asarray(tap_selection(), BF16)
    dma = pltpu.SemaphoreType.DMA
    return pl.pallas_call(
        forecast_kernel,
        out_shape=(
            jax.ShapeDtypeStruct((CELLS, MEM), BF16),
            jax.ShapeDtypeStruct((SUMMED, 128), F32),
        ),
        in_specs=[pl.BlockSpec(memory_space=pltpu.HBM)] * 9,
        out_specs=(pl.BlockSpec(memory_space=pltpu.HBM), VMEM),
        scratch_shapes=[
            pltpu.VMEM((CELLS, MEM), BF16),
            pltpu.VMEM((2, CZ, CX, CY, MEM), BF16),
            pltpu.VMEM((CZ, CX, CY), jnp.int32),
            pltpu.VMEM((OUTS, TAPS, 256), BF16),
            pltpu.VMEM((CH, TAPS), BF16),
            pltpu.SMEM((CH,), F32),
            pltpu.SMEM((CH,), F32),
            pltpu.SMEM((OBS,), jnp.int32),
            pltpu.VMEM((1, OBS), F32),
            pltpu.VMEM((1, OBS), F32),
            dma((10,)),
            pltpu.VMEM(((ROWS + 4) * PITCH, 128), F32),
            pltpu.VMEM(((ROWS + 4) * PITCH, 128), F32),
            pltpu.VMEM((OUTS * CH, 128), F32),
            pltpu.VMEM((OUTS * CH, 128), F32),
            pltpu.VMEM((OUTS * CH, 256), BF16),
            pltpu.VMEM((CELLS, 128), F32),
            pltpu.VMEM((CELLS, 128), F32),
            pltpu.VMEM((OBS, MEM), F32),
            pltpu.VMEM((SUMMED, 128), F32),
            pltpu.VMEM((2, 2, 4, CY, MEM), BF16),
            pltpu.VMEM((2, 2, 4, CY, MEM), BF16),
            pltpu.VMEM((CY // 4, MEM), BF16),
            pltpu.VMEM((CY // 4, MEM), BF16),
            dma((56,)),
            dma((2, 2)),
            dma((2, 2)),
            dma((2, 2, 2)),
            dma((2,)),
            pltpu.VMEM((8, 8 * TILES, 128), F32),
            pltpu.VMEM((8, 8, 128), F32),
            pltpu.VMEM((16, 8, 128), F32),
            pltpu.VMEM((8 * TILES, 128), F32),
            pltpu.VMEM((8, 128), F32),
            pltpu.VMEM((8 * TILES, 128), F32),
        ]
        + [dma((n,)) for n in (8, 8, 8, 8, 16, 16, 8, 8, 8, 8)],
        compiler_params=pltpu.CompilerParams(
            collective_id=1, has_side_effects=True, vmem_limit_bytes=63 << 20
        ),
        name="forecast",
    )(
        fields, mask, chosen, kernel.T, bias, read, cells,
        values.reshape(1, OBS), sigma.reshape(1, OBS),
    )


def total(
    part, out, from_a, from_b, from_c, sum_a, sum_b, whole,
    send_a, recv_a, send_b, recv_b, send_c, recv_c, send_d, recv_d, send_e, recv_e,
):
    cores = lax.axis_index("cores")
    face = lax.axis_index("face")
    a = lax.rem(cores, 8)
    y = lax.rem(cores // 8, 8)
    high = cores // 64
    z = high * 8 + face

    def peer_a(d):
        return (cores - a + lax.rem(a + d, 8), face)

    def peer_b(d):
        return (high * 64 + lax.rem(y + d, 8) * 8 + a, face)

    def peer_c(d):
        other = lax.rem(z + d, 16)
        return (other // 8 * 64 + lax.rem(cores, 64), lax.rem(other, 8))

    def greet(barrier):
        for d in range(1, 8):
            pl.semaphore_signal(barrier, inc=1, device_id=peer_a(d), device_id_type=MESH)
            pl.semaphore_signal(barrier, inc=1, device_id=peer_b(d), device_id_type=MESH)
        for d in range(1, 16):
            pl.semaphore_signal(barrier, inc=1, device_id=peer_c(d), device_id_type=MESH)

    def sum_over_devices():
        def rows(index, size):
            return pl.ds(pl.multiple_of(index * size, size), size)

        copies = []

        def launch(condition, copy):
            copies.append((condition, copy))
            if condition is None:
                copy.start()
            else:
                pl.when(condition)(copy.start)

        def make(src, dst, sems, d, peer):
            return pltpu.make_async_remote_copy(
                src_ref=src, dst_ref=dst, send_sem=sems[0].at[d], recv_sem=sems[1].at[d],
                device_id=peer, device_id_type=MESH,
            )

        eighth = 8 * TILES
        owner = y < TILES
        tile = jnp.minimum(y, TILES - 1)
        first = []
        for d in range(1, 8):
            copy = make(part.at[rows(lax.rem(a + d, 8), eighth), :], from_a.at[d], (send_a, recv_a), d, peer_a(d))
            launch(None, copy)
            first.append(copy)
        value = part[rows(a, eighth), :]
        for d in range(1, 8):
            first[d - 1].wait_recv()
            value = value + from_a[d]
        sum_a[...] = value
        second = []
        for d in range(1, 8):
            other = lax.rem(y + d, 8)
            copy = make(sum_a.at[rows(jnp.minimum(other, TILES - 1), 8), :], from_b.at[d], (send_b, recv_b), d, peer_b(d))
            launch(other < TILES, copy)
            second.append(copy)

        def add_tiles():
            value = sum_a[rows(tile, 8), :]
            for d in range(1, 8):
                second[d - 1].wait_recv()
                value = value + from_b[d]
            sum_b[...] = value

        pl.when(owner)(add_tiles)
        third = []
        for d in range(1, 16):
            copy = make(sum_b, from_c.at[d], (send_c, recv_c), d, peer_c(d))
            launch(owner, copy)
            third.append(copy)
        mine = whole.at[rows(tile, 8), :]

        def add_pieces():
            value = sum_b[...]
            for d in range(1, 16):
                third[d - 1].wait_recv()
                value = value + from_c[d]
            mine[...] = value

        pl.when(owner)(add_pieces)
        for d in range(1, 8):
            launch(owner, make(mine, mine, (send_d, recv_d), d, peer_b(d)))
        for d in range(1, 8):
            other = lax.rem(y + 8 - d, 8)
            there = whole.at[rows(jnp.minimum(other, TILES - 1), 8), :]
            pl.when(other < TILES)(make(there, there, (send_d, recv_d), d, peer_b(d)).wait_recv)
        place = out.at[rows(a, eighth), :]
        last = []
        for d in range(1, 8):
            copy = make(whole, place, (send_e, recv_e), d, peer_a(d))
            launch(None, copy)
            last.append(copy)
        place[...] = whole[...]
        for d in range(1, 8):
            last[d - 1].wait_recv()
        for condition, copy in copies:
            if condition is None:
                copy.wait_send()
            else:
                pl.when(condition)(copy.wait_send)

    return greet, sum_over_devices


PEERS = 7 + 7 + 15


def inverse_factor(gram):
    size = gram.shape[0]
    row_index = lax.broadcasted_iota(jnp.int32, (size, size), 0)
    column_index = lax.broadcasted_iota(jnp.int32, (size, size), 1)
    odd = lax.rem(row_index[:, 0:1], 2) == 1
    parts = [gram, jnp.where(row_index == column_index, 1.0, 0.0)]

    def wide(column):
        return jnp.broadcast_to(column, (column.shape[0], size))

    def down(block):
        return jnp.concatenate([block[-1:], block[:-1]], axis=0)

    finished = [[], []]
    for i in range(0, size, 8):
        more = i + 8 < size
        rows = [[part[q : q + 1, :] for q in range(8)] for part in parts]
        columns = [wide(parts[0][8:, i + q : i + q + 1]) for q in range(8)] if more else []
        entry = {
            (p, q): wide(rows[0][p][:, i + q : i + q + 1]) for p in range(8) for q in range(p, 8)
        }
        scaled = [[], []]
        for p in range(0, 8, 2):
            n = p + 1
            inverse_det = 1.0 / (entry[p, p] * entry[n, n] - entry[p, n] * entry[p, n])
            m00, m01, m11 = (
                entry[n, n] * inverse_det, -entry[p, n] * inverse_det, entry[p, p] * inverse_det
            )
            for own, out in zip(rows, scaled):
                out.append(m00 * own[p] + m01 * own[n])
                out.append(m01 * own[p] + m11 * own[n])
            for q in range(p + 2, 8):
                x0 = m00 * entry[p, q] + m01 * entry[n, q]
                x1 = m01 * entry[p, q] + m11 * entry[n, q]
                for t in range(q, 8):
                    entry[q, t] = entry[q, t] - (x0 * entry[p, t] + x1 * entry[n, t])
                for own in rows:
                    own[q] = own[q] - (x0 * own[p] + x1 * own[n])
                if more:
                    columns[q] = columns[q] - (columns[p] * x0 + columns[n] * x1)
        for half in range(2):
            finished[half].append(jnp.concatenate(rows[half], axis=0))
            if more:
                terms = [column * row for column, row in zip(columns, scaled[half])]
                parts[half] = parts[half][8:] - (
                    ((terms[0] + terms[1]) + (terms[2] + terms[3]))
                    + ((terms[4] + terms[5]) + (terms[6] + terms[7]))
                )
    left, right = (jnp.concatenate(blocks, axis=0) for blocks in finished)
    diagonal = jnp.sum(jnp.where(row_index == column_index, left, 0.0), axis=1, keepdims=True)
    beside = jnp.sum(jnp.where(row_index - 1 == column_index, left, 0.0), axis=1, keepdims=True)
    ratio = jnp.where(odd, beside / down(diagonal), 0.0)
    pivots = diagonal - ratio * beside
    return (right - ratio * down(right)) * (1.0 / jnp.sqrt(pivots))


LEAF = 128


def product(left, right, contracted):
    return lax.dot_general(
        left, right, (contracted, ((), ())), precision=HIGHEST, preferred_element_type=F32
    )


def inverse_lower(first, corner, last):
    lower_first = inverse_whole(first)
    upper = product(lower_first, corner, ((1,), (1,)))
    joined = product(upper, lower_first, ((0,), (0,)))
    lower_last = inverse_whole(last - product(upper, upper, ((0,), (0,))))
    return jnp.concatenate(
        [
            jnp.concatenate([lower_first, jnp.zeros_like(lower_first)], axis=1),
            jnp.concatenate([-product(lower_last, joined, ((1,), (0,))), lower_last], axis=1),
        ],
        axis=0,
    )


def inverse_whole(gram):
    half = gram.shape[0] // 2
    if gram.shape[0] <= LEAF:
        return inverse_factor(gram)
    return inverse_lower(gram[:half, :half], gram[half:, :half], gram[half:, half:])


def analysis_kernel(
    gram_hbm, fields_hbm, sat_hbm, out_hbm,
    gram_in, fields, sat, out, load_sem, store_sem,
):
    loads = [
        pltpu.make_async_copy(src, dst, load_sem.at[n])
        for n, (src, dst) in enumerate(((gram_hbm, gram_in), (fields_hbm, fields), (sat_hbm, sat)))
    ]
    for load in loads:
        load.start()
    loads[0].wait()
    first, corner, last, coeff = unpacked(gram_in[...])
    row, column = half_indices()
    identity = jnp.where(row == column, 1.0, 0.0)
    low = inverse_lower(first + identity, corner, last + identity)
    half_way = jnp.sum(low * coeff, axis=1, keepdims=True)
    weights = jnp.sum(low * half_way, axis=0, keepdims=True)
    mixing_t = (low + weights).astype(BF16)

    def update(state):
        state = state.astype(F32)
        mean = jnp.sum(state, axis=1, keepdims=True) * (1.0 / MEM)
        moved = lax.dot_general(
            (state - mean).astype(BF16), mixing_t, (((1,), (1,)), ((), ())),
            preferred_element_type=F32,
        )
        return (mean + moved).astype(BF16)

    loads[1].wait()
    loads[2].wait()
    stores = []
    for z in range(CZ):
        for x in range(CX):
            for f in range(3):
                out[f, z, x] = update(fields[f, z, x] if f < 2 else sat[z, x])
            store = pltpu.make_async_copy(
                out.at[:, z, x], out_hbm.at[:, z, x], store_sem.at[z * CX + x]
            )
            store.start()
            stores.append(store)
    for store in stores:
        store.wait()


def analysis(gram, fields, sat):
    return pl.pallas_call(
        analysis_kernel,
        out_shape=jax.ShapeDtypeStruct((3,) + fields.shape[1:], BF16),
        in_specs=[pl.BlockSpec(memory_space=pltpu.HBM)] * 3,
        out_specs=pl.BlockSpec(memory_space=pltpu.HBM),
        scratch_shapes=[
            pltpu.VMEM(gram.shape, F32),
            pltpu.VMEM(fields.shape, BF16),
            pltpu.VMEM(sat.shape, BF16),
            pltpu.VMEM((3,) + fields.shape[1:], BF16),
            pltpu.SemaphoreType.DMA((3,)),
            pltpu.SemaphoreType.DMA((CZ * CX,)),
        ],
        compiler_params=pltpu.CompilerParams(vmem_limit_bytes=63 << 20),
        name="analysis",
    )(gram, fields, sat)


def shards(
    fields, pore_mask, conv_kernel, conv_bias, read_weight, obs_cells, obs_values, obs_sigma
):
    sat, summed = forecast(
        fields, pore_mask, conv_kernel, conv_bias, read_weight, obs_cells, obs_values, obs_sigma
    )
    return analysis(summed, fields, sat.reshape(CZ, CX, CY, MEM))


def solution(mesh):
    return jax.shard_map(
        shards,
        mesh=mesh,
        in_specs=(
            P(None, "cores", "face", None, None),
            P("cores", "face", None),
            P(),
            P(),
            P(),
            P(("cores", "face")),
            P(("cores", "face")),
            P(("cores", "face")),
        ),
        out_specs=P(None, "cores", "face", None, None),
        check_vma=False,
    )
```

```python
import functools
import math

import jax
import jax.numpy as jnp
import numpy as np
from jax import lax
from jax.experimental import pallas as pl
from jax.experimental.pallas import tpu as pltpu
from jax.sharding import PartitionSpec as P

MESH = pl.DeviceIdType.MESH
HIGHEST = lax.Precision.HIGHEST
F32 = jnp.float32
BF16 = jnp.bfloat16
VMEM = pl.BlockSpec(memory_space=pltpu.VMEM)
SMEM = pl.BlockSpec(memory_space=pltpu.SMEM)

CH = 32
CZ, CX, CY, MEM = 2, 4, 128, 256
CELLS = CZ * CX * CY
OBS = 64
TAPS = 54
ROWS = 2 * (CZ + 2) * (CX + 2)
SPAN = 40
PITCH = 144
HEAD = 8
OUTS = 4 * CX
DEPTH = 6 * SPAN
ROOT = math.sqrt(MEM - 1)
HALF = MEM // 2
TILES = 5
SUMMED = 8 * 8 * TILES


def tap_selection():
    chosen = np.zeros((OUTS, TAPS, 256), np.float32)
    for yo in range(4):
        for xo in range(CX):
            for f in range(2):
                for a in range(3):
                    for b in range(3):
                        for c in range(3):
                            row = (2 * a + f) * (CX + 2) + xo + b
                            chosen[
                                yo * CX + xo, 27 * f + 9 * a + 3 * b + c, (yo + c) * SPAN + row
                            ] = 1.0
    return chosen


def exchange(
    fields, zh, xh, hop_1, hop_2, sent, z_sem, edge_sem, corner_sem, hop_sem, greet_more, more, meanwhile
):
    cores = lax.axis_index("cores")
    face = lax.axis_index("face")
    core = lax.rem(cores, 2)
    x_chip = lax.rem(cores // 2, 4)
    y_chip = lax.rem(cores // 8, 8)
    high = cores // 64
    above, below = lax.rem(cores + 1, 128), lax.rem(cores + 127, 128)
    top, bottom = lax.rem(cores, 64) == 63, lax.rem(cores, 64) == 0
    not_top, not_bottom = jnp.logical_not(top), jnp.logical_not(bottom)
    has_left, has_right = face > 0, face < 7
    partner = lax.rem(cores + 64, 128)
    first = high * 64 + core * 63
    last = high * 64 + 63 - core * 63
    is_first = cores == first
    later = jnp.logical_not(is_first)
    sends_right = lax.rem(y_chip, 4) == 3
    sends_left = lax.rem(y_chip, 4) == 0

    def both(*conditions):
        return functools.reduce(jnp.logical_and, conditions)

    barrier = pltpu.get_barrier_semaphore()

    def greet(condition, *peers):
        def signal():
            for peer in peers:
                pl.semaphore_signal(barrier, inc=1, device_id=peer, device_id_type=MESH)

        if condition is None:
            signal()
        else:
            pl.when(condition)(signal)

    def columns(core_of, rows, face_of):
        return [(high * 64 + j * 8 + i * 2 + core_of, face_of) for j in rows for i in range(4)]

    greet_more(barrier)
    greet(None, (partner, face))
    greet(later, (first, face))
    greet(not_bottom, (below, face))
    greet(not_top, (above, face))
    greet(has_left, (cores, face - 1))
    greet(has_right, (cores, face + 1))
    for end, core_of in ((bottom, 1), (top, 0)):
        greet(end, *columns(core_of, range(8), face))
        greet(both(end, has_left), *columns(core_of, (3, 7), face - 1))
        greet(both(end, has_right), *columns(core_of, (0, 4), face + 1))

    def one(condition):
        return jnp.where(condition, 1, 0)

    expected = (
        2
        + more
        + one(not_top)
        + one(not_bottom)
        + one(has_left)
        + one(has_right)
        + one(both(sends_right, has_right))
        + one(both(sends_left, has_left))
        + 31 * one(is_first)
    )
    pl.semaphore_wait(barrier, expected)

    started = []

    def send(condition, src, dst, arrived, *peer):
        copy = pltpu.make_async_remote_copy(
            src_ref=src, dst_ref=dst, send_sem=sent.at[len(started)], recv_sem=arrived,
            device_id=peer, device_id_type=MESH,
        )
        started.append((condition, copy))
        if condition is None:
            copy.start()
        else:
            pl.when(condition)(copy.start)

    def arrival(dst, arrived, *peer):
        return pltpu.make_async_remote_copy(
            src_ref=dst, dst_ref=dst, send_sem=sent.at[0], recv_sem=arrived,
            device_id=peer, device_id_type=MESH,
        )

    part = CY // 4

    def rows(quarter):
        return pl.ds(pl.multiple_of(quarter * part, part), part)

    def piece(j, i):
        return fields.at[j // 4, core, lax.rem(j, 4), rows(i), :]

    for n in range(31):
        at = n + 1 - core
        j, i = at // 4, lax.rem(at, 4)
        send(is_first, piece(j, i), hop_1, hop_sem.at[0], high * 64 + at * 2 + core, face)
    send(is_first, piece(y_chip, x_chip), hop_2, hop_sem.at[1], partner, face)
    for side, x, condition, peer in (
        (0, CX - 1, has_right, face + 1),
        (1, 0, has_left, face - 1),
    ):
        for f in range(2):
            send(condition, fields.at[f, :, x], xh.at[side, f, pl.ds(1, CZ)], edge_sem.at[side, f], cores, peer)
    pl.when(later)(arrival(hop_1, hop_sem.at[0], first, face).wait_recv)
    send(later, hop_1, hop_2, hop_sem.at[1], partner, face)
    for f in range(2):
        send(not_top, fields.at[f, CZ - 1], zh.at[0, f], z_sem.at[0, f], above, face)
        send(not_bottom, fields.at[f, 0], zh.at[1, f], z_sem.at[1, f], below, face)
    meanwhile()
    for side, condition in ((0, has_left), (1, has_right)):
        for f in range(2):
            pl.when(condition)(
                arrival(xh.at[side, f, pl.ds(1, CZ)], edge_sem.at[side, f], partner, face).wait_recv
            )
            send(both(condition, not_top), xh.at[side, f, CZ], xh.at[side, f, 0], corner_sem.at[side, f, 0], above, face)
            send(both(condition, not_bottom), xh.at[side, f, 1], xh.at[side, f, CZ + 1], corner_sem.at[side, f, 1], below, face)
    arrival(hop_2, hop_sem.at[1], partner, face).wait_recv()
    f, x = y_chip // 4, lax.rem(y_chip, 4)
    side = 1 - core
    plane = 3 * side
    send(None, hop_2, zh.at[side, f, x, rows(x_chip), :], z_sem.at[side, f], last, face)
    for to, condition, peer in (
        (0, both(sends_right, has_right), face + 1),
        (1, both(sends_left, has_left), face - 1),
    ):
        send(condition, hop_2, xh.at[to, f, plane, rows(x_chip), :], corner_sem.at[to, f, side], last, peer)

    def wait_side(end):
        for f in range(2):
            arrival(zh.at[end, f], z_sem.at[end, f], partner, face).wait_recv()

        def wait_corners(side):
            for f in range(2):
                arrival(xh.at[side, f, 3 * end], corner_sem.at[side, f, end], partner, face).wait_recv()

        pl.when(has_left)(functools.partial(wait_corners, 0))
        pl.when(has_right)(functools.partial(wait_corners, 1))

    def clear(side):
        xh[side] = jnp.zeros_like(xh[side])

    pl.when(jnp.logical_not(has_left))(functools.partial(clear, 0))
    pl.when(jnp.logical_not(has_right))(functools.partial(clear, 1))

    def finish():
        for condition, copy in started:
            if condition is None:
                copy.wait_send()
            else:
                pl.when(condition)(copy.wait_send)

    return wait_side, finish


def half_indices():
    shape = (HALF, HALF)
    return lax.broadcasted_iota(jnp.int32, shape, 0), lax.broadcasted_iota(jnp.int32, shape, 1)


def packed(gram, coeff):
    row, column = half_indices()
    last = gram[HALF:, HALF:]
    diagonal = jnp.sum(jnp.where(row == column, last, 0.0), axis=0, keepdims=True)
    return jnp.concatenate(
        [
            gram[HALF:, :HALF],
            jnp.where(row >= column, gram[:HALF, :HALF], last),
            diagonal,
            coeff[:, :HALF],
            coeff[:, HALF:],
            jnp.zeros((SUMMED - MEM - 3, HALF), F32),
        ],
        axis=0,
    )


def unpacked(rows):
    row, column = half_indices()
    corner = rows[:HALF]
    joint = rows[HALF:MEM]
    turned = joint.T
    first = jnp.where(row >= column, joint, turned)
    last = jnp.where(row == column, rows[MEM : MEM + 1], jnp.where(row < column, joint, turned))
    coeff = jnp.concatenate([rows[MEM + 1 : MEM + 2], rows[MEM + 2 : MEM + 3]], axis=1)
    return first, corner, last, coeff


def forecast_kernel(
    fields, mask_in, chosen_in, kernel_in, bias_in, read_in, cells_in, values_in, sigma_in,
    sat_hbm, total_out,
    sat_out, fields_here, mask, chosen, kernel_t, bias, read, cells, values, sigma, load_sem,
    padded_0, padded_1, rows_0, rows_1, weights, sat_0, sat_1, predicted, part,
    zh, xh, hop_1, hop_2, sent, z_sem, edge_sem, corner_sem, hop_sem, *total_scratch,
):
    loads = [
        pltpu.make_async_copy(src, dst, load_sem.at[n])
        for n, (src, dst) in enumerate(
            (
                (fields, fields_here), (mask_in, mask), (chosen_in, chosen), (kernel_in, kernel_t),
                (bias_in, bias), (read_in, read), (cells_in, cells), (values_in, values),
                (sigma_in, sigma),
            )
        )
    ]
    for load in loads:
        load.start()

    def place(row, block):
        block = block.astype(F32)
        own = pl.ds(pl.multiple_of(row * PITCH + HEAD, 8), CY)
        padded_0[own, :] = block[:, 0:128]
        padded_1[own, :] = block[:, 128:256]

    def slot(f, z, x):
        return (2 * z + f) * (CX + 2) + x

    def prepare():
        for load in loads:
            load.wait()
        own_rows()
        make_weights()

    def own_rows():
        blank = jnp.zeros((8, 128), F32)
        for row in range(ROWS):
            for padded in (padded_0, padded_1):
                padded[pl.ds(row * PITCH, 8), :] = blank
                padded[pl.ds(row * PITCH + HEAD + CY, 8), :] = blank
        for padded in (padded_0, padded_1):
            padded[ROWS * PITCH :, :] = jnp.zeros((4 * PITCH, 128), F32)
        for f in range(2):
            for x in range(CX):
                for z in range(CZ):
                    place(slot(f, z + 1, x + 1), fields_here[f, z, x])

    def make_weights():
        taps = kernel_t[...]
        for out in range(OUTS):
            piece = jnp.dot(taps, chosen[out], preferred_element_type=F32)
            rows_0[pl.ds(out * CH, CH), :] = piece[:, 0:128]
            rows_1[pl.ds(out * CH, CH), :] = piece[:, 128:256]
        lane = lax.broadcasted_iota(jnp.int32, (OUTS, 16), 1)
        for c in range(CH):
            own = pl.ds(c * OUTS, OUTS)
            every = pl.ds(c, OUTS, stride=CH)
            weights[own, 0:128] = (rows_0[every, :] * 0.5).astype(BF16)
            weights[own, 128:256] = (rows_1[every, :] * 0.5).astype(BF16)
            whole = jnp.full((OUTS, 16), bias[c] * 0.5, F32)
            high = whole.astype(BF16).astype(F32)
            middle = (whole - high).astype(BF16).astype(F32)
            low = whole - high - middle
            split = jnp.where(
                lane == 0, high, jnp.where(lane == 1, middle, jnp.where(lane == 2, low, 0.0))
            )
            weights[own, DEPTH : DEPTH + 16] = split.astype(BF16)

    greet_total, sum_over_devices = total(part, total_out, *total_scratch)
    wait_side, finish = exchange(
        fields, zh, xh, hop_1, hop_2, sent, z_sem, edge_sem, corner_sem, hop_sem,
        greet_total, PEERS, prepare,
    )

    def place_side(end):
        for f in range(2):
            for x in range(CX):
                place(slot(f, 3 * end, x + 1), zh[end, f, x])
            place(slot(f, 3 * end, 0), xh[0, f, 3 * end])
            place(slot(f, 3 * end, CX + 1), xh[1, f, 3 * end])

    ones = jnp.ones((256 - DEPTH, 128), F32)

    def step(plane, t, carry):
        halves = []
        start = plane * (2 * (CX + 2) * PITCH) + HEAD - 1 + 4 * t
        for padded in (padded_0, padded_1):
            rows = [padded[pl.ds(start + q, SPAN, stride=PITCH), :] for q in range(6)]
            halves.append(jnp.concatenate(rows + [ones], axis=0).astype(BF16))
        inputs = jnp.concatenate(halves, axis=1)
        half = jnp.dot(weights[...], inputs, preferred_element_type=F32)
        total = jnp.zeros((OUTS, MEM), F32)
        for c in range(CH):
            h = half[c * OUTS : (c + 1) * OUTS]
            total = total + read[c] * (h + h * jnp.tanh(h))
        level = 0.5 + 0.5 * jnp.tanh(0.5 * total)
        for yo in range(4):
            cells_of = pl.ds(plane * (CX * CY) + 4 * t + yo, CX, stride=CY)
            sat_0[cells_of, :] = level[yo * CX : yo * CX + CX, 0:128]
            sat_1[cells_of, :] = level[yo * CX : yo * CX + CX, 128:256]
        return carry

    core = lax.rem(lax.axis_index("cores"), 2)
    for f in range(2):
        for z in range(1, CZ + 1):
            place(slot(f, z, 0), xh[0, f, z])
            place(slot(f, z, CX + 1), xh[1, f, z])
    for plane in (1 - core, core):
        wait_side(plane)
        place_side(plane)
        lax.fori_loop(0, CY // 4, functools.partial(step, plane), 0, unroll=16)

    columns = jnp.concatenate([mask[0], mask[1]], axis=0).astype(F32).T
    for zx in range(CZ * CX):
        own = pl.ds(zx * CY, CY)
        for lane_0, sat in ((0, sat_0), (128, sat_1)):
            rounded = (sat[own, :] * columns[:, zx : zx + 1]).astype(BF16)
            sat_out[own, lane_0 : lane_0 + 128] = rounded
            sat[own, :] = rounded.astype(F32)

    store = pltpu.make_async_copy(sat_out, sat_hbm, load_sem.at[9])
    store.start()

    for o in range(OBS):
        predicted[pl.ds(o, 1), 0:128] = sat_0[pl.ds(cells[o], 1), :]
        predicted[pl.ds(o, 1), 128:256] = sat_1[pl.ds(cells[o], 1), :]
    diagonal = lax.broadcasted_iota(jnp.int32, (OBS, OBS), 0) == lax.broadcasted_iota(
        jnp.int32, (OBS, OBS), 1
    )

    def column(row):
        return jnp.sum(jnp.where(diagonal, row[...], 0.0), axis=1, keepdims=True)

    inverse_sigma = 1.0 / column(sigma)
    pred = predicted[...]
    center = jnp.sum(pred, axis=1, keepdims=True) * (1.0 / MEM)
    scaled = (pred - center) * (inverse_sigma * (1.0 / ROOT))
    innovation = (column(values) - center) * inverse_sigma
    gram = lax.dot_general(
        scaled, scaled, (((0,), (0,)), ((), ())), precision=HIGHEST, preferred_element_type=F32
    )
    coeff = jnp.sum(scaled * innovation, axis=0, keepdims=True) * (1.0 / ROOT)
    part[...] = packed(gram, coeff)
    sum_over_devices()
    finish()
    store.wait()


def forecast(fields, mask, kernel, bias, read, cells, values, sigma):
    chosen = jnp.asarray(tap_selection(), BF16)
    dma = pltpu.SemaphoreType.DMA
    return pl.pallas_call(
        forecast_kernel,
        out_shape=(
            jax.ShapeDtypeStruct((CELLS, MEM), BF16),
            jax.ShapeDtypeStruct((SUMMED, 128), F32),
        ),
        in_specs=[pl.BlockSpec(memory_space=pltpu.HBM)] * 9,
        out_specs=(pl.BlockSpec(memory_space=pltpu.HBM), VMEM),
        scratch_shapes=[
            pltpu.VMEM((CELLS, MEM), BF16),
            pltpu.VMEM((2, CZ, CX, CY, MEM), BF16),
            pltpu.VMEM((CZ, CX, CY), jnp.int32),
            pltpu.VMEM((OUTS, TAPS, 256), BF16),
            pltpu.VMEM((CH, TAPS), BF16),
            pltpu.SMEM((CH,), F32),
            pltpu.SMEM((CH,), F32),
            pltpu.SMEM((OBS,), jnp.int32),
            pltpu.VMEM((1, OBS), F32),
            pltpu.VMEM((1, OBS), F32),
            dma((10,)),
            pltpu.VMEM(((ROWS + 4) * PITCH, 128), F32),
            pltpu.VMEM(((ROWS + 4) * PITCH, 128), F32),
            pltpu.VMEM((OUTS * CH, 128), F32),
            pltpu.VMEM((OUTS * CH, 128), F32),
            pltpu.VMEM((OUTS * CH, 256), BF16),
            pltpu.VMEM((CELLS, 128), F32),
            pltpu.VMEM((CELLS, 128), F32),
            pltpu.VMEM((OBS, MEM), F32),
            pltpu.VMEM((SUMMED, 128), F32),
            pltpu.VMEM((2, 2, 4, CY, MEM), BF16),
            pltpu.VMEM((2, 2, 4, CY, MEM), BF16),
            pltpu.VMEM((CY // 4, MEM), BF16),
            pltpu.VMEM((CY // 4, MEM), BF16),
            dma((56,)),
            dma((2, 2)),
            dma((2, 2)),
            dma((2, 2, 2)),
            dma((2,)),
            pltpu.VMEM((8, 8 * TILES, 128), F32),
            pltpu.VMEM((8, 8, 128), F32),
            pltpu.VMEM((16, 8, 128), F32),
            pltpu.VMEM((8 * TILES, 128), F32),
            pltpu.VMEM((8, 128), F32),
            pltpu.VMEM((8 * TILES, 128), F32),
        ]
        + [dma((n,)) for n in (8, 8, 8, 8, 16, 16, 8, 8, 8, 8)],
        compiler_params=pltpu.CompilerParams(
            collective_id=1, has_side_effects=True, vmem_limit_bytes=63 << 20
        ),
        name="forecast",
    )(
        fields, mask, chosen, kernel.T, bias, read, cells,
        values.reshape(1, OBS), sigma.reshape(1, OBS),
    )


def total(
    part, out, from_a, from_b, from_c, sum_a, sum_b, whole,
    send_a, recv_a, send_b, recv_b, send_c, recv_c, send_d, recv_d, send_e, recv_e,
):
    cores = lax.axis_index("cores")
    face = lax.axis_index("face")
    a = lax.rem(cores, 8)
    y = lax.rem(cores // 8, 8)
    high = cores // 64
    z = high * 8 + face

    def peer_a(d):
        return (cores - a + lax.rem(a + d, 8), face)

    def peer_b(d):
        return (high * 64 + lax.rem(y + d, 8) * 8 + a, face)

    def peer_c(d):
        other = lax.rem(z + d, 16)
        return (other // 8 * 64 + lax.rem(cores, 64), lax.rem(other, 8))

    def greet(barrier):
        for d in range(1, 8):
            pl.semaphore_signal(barrier, inc=1, device_id=peer_a(d), device_id_type=MESH)
            pl.semaphore_signal(barrier, inc=1, device_id=peer_b(d), device_id_type=MESH)
        for d in range(1, 16):
            pl.semaphore_signal(barrier, inc=1, device_id=peer_c(d), device_id_type=MESH)

    def sum_over_devices():
        def rows(index, size):
            return pl.ds(pl.multiple_of(index * size, size), size)

        copies = []

        def launch(condition, copy):
            copies.append((condition, copy))
            if condition is None:
                copy.start()
            else:
                pl.when(condition)(copy.start)

        def make(src, dst, sems, d, peer):
            return pltpu.make_async_remote_copy(
                src_ref=src, dst_ref=dst, send_sem=sems[0].at[d], recv_sem=sems[1].at[d],
                device_id=peer, device_id_type=MESH,
            )

        eighth = 8 * TILES
        owner = y < TILES
        tile = jnp.minimum(y, TILES - 1)
        first = []
        for d in range(1, 8):
            copy = make(part.at[rows(lax.rem(a + d, 8), eighth), :], from_a.at[d], (send_a, recv_a), d, peer_a(d))
            launch(None, copy)
            first.append(copy)
        value = part[rows(a, eighth), :]
        for d in range(1, 8):
            first[d - 1].wait_recv()
            value = value + from_a[d]
        sum_a[...] = value
        second = []
        for d in range(1, 8):
            other = lax.rem(y + d, 8)
            copy = make(sum_a.at[rows(jnp.minimum(other, TILES - 1), 8), :], from_b.at[d], (send_b, recv_b), d, peer_b(d))
            launch(other < TILES, copy)
            second.append(copy)

        def add_tiles():
            value = sum_a[rows(tile, 8), :]
            for d in range(1, 8):
                second[d - 1].wait_recv()
                value = value + from_b[d]
            sum_b[...] = value

        pl.when(owner)(add_tiles)
        third = []
        for d in range(1, 16):
            copy = make(sum_b, from_c.at[d], (send_c, recv_c), d, peer_c(d))
            launch(owner, copy)
            third.append(copy)
        mine = whole.at[rows(tile, 8), :]

        def add_pieces():
            value = sum_b[...]
            for d in range(1, 16):
                third[d - 1].wait_recv()
                value = value + from_c[d]
            mine[...] = value

        pl.when(owner)(add_pieces)
        for d in range(1, 8):
            launch(owner, make(mine, mine, (send_d, recv_d), d, peer_b(d)))
        for d in range(1, 8):
            other = lax.rem(y + 8 - d, 8)
            there = whole.at[rows(jnp.minimum(other, TILES - 1), 8), :]
            pl.when(other < TILES)(make(there, there, (send_d, recv_d), d, peer_b(d)).wait_recv)
        place = out.at[rows(a, eighth), :]
        last = []
        for d in range(1, 8):
            copy = make(whole, place, (send_e, recv_e), d, peer_a(d))
            launch(None, copy)
            last.append(copy)
        place[...] = whole[...]
        for d in range(1, 8):
            last[d - 1].wait_recv()
        for condition, copy in copies:
            if condition is None:
                copy.wait_send()
            else:
                pl.when(condition)(copy.wait_send)

    return greet, sum_over_devices


PEERS = 7 + 7 + 15


def inverse_factor(gram):
    size = gram.shape[0]
    row_index = lax.broadcasted_iota(jnp.int32, (size, size), 0)
    column_index = lax.broadcasted_iota(jnp.int32, (size, size), 1)
    odd = lax.rem(row_index[:, 0:1], 2) == 1
    parts = [gram, jnp.where(row_index == column_index, 1.0, 0.0)]

    def wide(column):
        return jnp.broadcast_to(column, (column.shape[0], size))

    def down(block):
        return jnp.concatenate([block[-1:], block[:-1]], axis=0)

    finished = [[], []]
    for i in range(0, size, 8):
        more = i + 8 < size
        rows = [[part[q : q + 1, :] for q in range(8)] for part in parts]
        columns = [wide(parts[0][8:, i + q : i + q + 1]) for q in range(8)] if more else []
        entry = {
            (p, q): wide(rows[0][p][:, i + q : i + q + 1]) for p in range(8) for q in range(p, 8)
        }
        scaled = [[], []]
        for p in range(0, 8, 2):
            n = p + 1
            inverse_det = 1.0 / (entry[p, p] * entry[n, n] - entry[p, n] * entry[p, n])
            m00, m01, m11 = (
                entry[n, n] * inverse_det, -entry[p, n] * inverse_det, entry[p, p] * inverse_det
            )
            for own, out in zip(rows, scaled):
                out.append(m00 * own[p] + m01 * own[n])
                out.append(m01 * own[p] + m11 * own[n])
            for q in range(p + 2, 8):
                x0 = m00 * entry[p, q] + m01 * entry[n, q]
                x1 = m01 * entry[p, q] + m11 * entry[n, q]
                for t in range(q, 8):
                    entry[q, t] = entry[q, t] - (x0 * entry[p, t] + x1 * entry[n, t])
                for own in rows:
                    own[q] = own[q] - (x0 * own[p] + x1 * own[n])
                if more:
                    columns[q] = columns[q] - (columns[p] * x0 + columns[n] * x1)
        for half in range(2):
            finished[half].append(jnp.concatenate(rows[half], axis=0))
            if more:
                terms = [column * row for column, row in zip(columns, scaled[half])]
                parts[half] = parts[half][8:] - (
                    ((terms[0] + terms[1]) + (terms[2] + terms[3]))
                    + ((terms[4] + terms[5]) + (terms[6] + terms[7]))
                )
    left, right = (jnp.concatenate(blocks, axis=0) for blocks in finished)
    diagonal = jnp.sum(jnp.where(row_index == column_index, left, 0.0), axis=1, keepdims=True)
    beside = jnp.sum(jnp.where(row_index - 1 == column_index, left, 0.0), axis=1, keepdims=True)
    ratio = jnp.where(odd, beside / down(diagonal), 0.0)
    pivots = diagonal - ratio * beside
    return (right - ratio * down(right)) * (1.0 / jnp.sqrt(pivots))


LEAF = 128


def product(left, right, contracted):
    return lax.dot_general(
        left, right, (contracted, ((), ())), precision=HIGHEST, preferred_element_type=F32
    )


def inverse_lower(first, corner, last):
    lower_first = inverse_whole(first)
    upper = product(lower_first, corner, ((1,), (1,)))
    joined = product(upper, lower_first, ((0,), (0,)))
    lower_last = inverse_whole(last - product(upper, upper, ((0,), (0,))))
    return jnp.concatenate(
        [
            jnp.concatenate([lower_first, jnp.zeros_like(lower_first)], axis=1),
            jnp.concatenate([-product(lower_last, joined, ((1,), (0,))), lower_last], axis=1),
        ],
        axis=0,
    )


def inverse_whole(gram):
    half = gram.shape[0] // 2
    if gram.shape[0] <= LEAF:
        return inverse_factor(gram)
    return inverse_lower(gram[:half, :half], gram[half:, :half], gram[half:, half:])


def analysis_kernel(
    gram_hbm, fields_hbm, sat_hbm, out_hbm,
    gram_in, fields, sat, out, load_sem, store_sem,
):
    loads = [
        pltpu.make_async_copy(src, dst, load_sem.at[n])
        for n, (src, dst) in enumerate(((gram_hbm, gram_in), (fields_hbm, fields), (sat_hbm, sat)))
    ]
    for load in loads:
        load.start()
    loads[0].wait()
    first, corner, last, coeff = unpacked(gram_in[...])
    row, column = half_indices()
    identity = jnp.where(row == column, 1.0, 0.0)
    low = inverse_lower(first + identity, corner, last + identity)
    half_way = jnp.sum(low * coeff, axis=1, keepdims=True)
    weights = jnp.sum(low * half_way, axis=0, keepdims=True)
    mixing_t = (low + weights).astype(BF16)

    def update(state):
        state = state.astype(F32)
        mean = jnp.sum(state, axis=1, keepdims=True) * (1.0 / MEM)
        moved = lax.dot_general(
            (state - mean).astype(BF16), mixing_t, (((1,), (1,)), ((), ())),
            preferred_element_type=F32,
        )
        return (mean + moved).astype(BF16)

    loads[1].wait()
    loads[2].wait()
    stores = []
    for z in range(CZ):
        for x in range(CX):
            for f in range(3):
                out[f, z, x] = update(fields[f, z, x] if f < 2 else sat[z, x])
            store = pltpu.make_async_copy(
                out.at[:, z, x], out_hbm.at[:, z, x], store_sem.at[z * CX + x]
            )
            store.start()
            stores.append(store)
    for store in stores:
        store.wait()


def analysis(gram, fields, sat):
    return pl.pallas_call(
        analysis_kernel,
        out_shape=jax.ShapeDtypeStruct((3,) + fields.shape[1:], BF16),
        in_specs=[pl.BlockSpec(memory_space=pltpu.HBM)] * 3,
        out_specs=pl.BlockSpec(memory_space=pltpu.HBM),
        scratch_shapes=[
            pltpu.VMEM(gram.shape, F32),
            pltpu.VMEM(fields.shape, BF16),
            pltpu.VMEM(sat.shape, BF16),
            pltpu.VMEM((3,) + fields.shape[1:], BF16),
            pltpu.SemaphoreType.DMA((3,)),
            pltpu.SemaphoreType.DMA((CZ * CX,)),
        ],
        compiler_params=pltpu.CompilerParams(vmem_limit_bytes=63 << 20),
        name="analysis",
    )(gram, fields, sat)


def shards(
    fields, pore_mask, conv_kernel, conv_bias, read_weight, obs_cells, obs_values, obs_sigma
):
    sat, summed = forecast(
        fields, pore_mask, conv_kernel, conv_bias, read_weight, obs_cells, obs_values, obs_sigma
    )
    return analysis(summed, fields, sat.reshape(CZ, CX, CY, MEM))


def solution(mesh):
    return jax.shard_map(
        shards,
        mesh=mesh,
        in_specs=(
            P(None, "cores", "face", None, None),
            P("cores", "face", None),
            P(),
            P(),
            P(),
            P(("cores", "face")),
            P(("cores", "face")),
            P(("cores", "face")),
        ),
        out_specs=P(None, "cores", "face", None, None),
        check_vma=False,
    )
```
